256 devices in a mesh: row: 16 (over x_lo, y, core), col: 16 (over z, x_hi).
Axes of the slice: x: 4 (x_hi: 2, x_lo: 2; x = x_hi * 2 + x_lo), y: 4, z: 8, core: 2. Of those that a mesh axis runs over, the one named last changes fastest.
Arguments:
- block_vecs: float32 [16, 131072], P(None, ('col', 'row')), may hold values from -130 to 130
- direction: float32 [16, 131072], P(None, ('col', 'row')), may hold values from -130 to 130
- blocks: bfloat16 [1024, 32, 128, 128], P('col', 'row'), may hold values from 0 to 4
- block_cols: int32 [1024, 32], P('col', 'row'), may hold values from 0 to 1023, as said below
- live_counts: int32 [1024, 16], P('col', 'row'), may hold values from 1 to 2, as said below
Outputs:
- x_next: float32 [16, 131072], P(None, ('col', 'row'))
- reduced: float32 [48, 48], replicated
- residual: float32 [16, 131072], P(None, ('col', 'row'))
The draws below stay inside these ranges and needn't reach their ends.
Inputs may be any that keep to these rules, and one draw needn't show every extreme that they name: `block_cols`: A block column index g in slots 2 * r to 2 * r + 1 of any block row satisfies (g // 4) mod 16 == r. `live_counts`: every block row has 2 live slots in at least one segment.
All inputs are finite; a program needn't handle non-finite values.
Results may differ from the reference program's by a relative error of at most 0.0003.
Values sent between devices are 32-bit elements; how exact they have to be, the bound alone decides.
A program may use at most 64 MiB of HBM per device.

```python
import math
import jax
import jax.numpy as jnp
from jax import lax

W = 16
BS = 128
KT = 2
M = 512
ORDER = 131072
NBR = 1024
N_ROW = 16
N_COL = 16


def vector_draw(key):
    subkeys = jax.random.split(key, 3)
    position = jnp.arange(ORDER, dtype=jnp.float32) / ORDER
    rough = jax.random.uniform(subkeys[0], (ORDER,), jnp.float32)
    row_scale = 10.0 ** (0.5 * position + 0.5 * rough)
    col_scale = 10.0 ** (0.5 * jax.random.uniform(subkeys[1], (W, 1), jnp.float32))
    base = jax.random.normal(subkeys[2], (W, ORDER), jnp.float32)
    base = jnp.clip(base, -4.0, 4.0)
    return base * row_scale[None, :] * col_scale


def draw_block_vecs(key, part):
    return vector_draw(jax.random.fold_in(key, 11))


def draw_direction(key, part):
    return vector_draw(jax.random.fold_in(key, 23))


def draw_blocks(key, part):
    fan_total = BS * KT * N_ROW
    levels = jax.random.uniform(jax.random.fold_in(key, 71), (NBR, N_ROW * KT, BS, BS), jnp.float32)
    return (0.04 / math.sqrt(fan_total) * 100.0 ** levels).astype(jnp.bfloat16)


def draw_block_cols(key, part):
    subkeys = jax.random.split(jax.random.fold_in(key, 37), 4)
    per_span = M // BS
    slot_count = N_ROW * KT
    segment = jnp.arange(slot_count, dtype=jnp.int32) // KT
    group_index = jax.random.randint(subkeys[0], (NBR, slot_count), 0, N_COL)
    offset = jax.random.randint(subkeys[1], (NBR, slot_count), 0, per_span)
    columns = (group_index * N_ROW + segment[None, :]) * per_span + offset
    low_row = jax.random.randint(subkeys[2], (), 0, NBR)
    high_row = jax.random.randint(subkeys[3], (), 0, NBR)
    columns = columns.at[low_row, 0].set(0)
    columns = columns.at[high_row, slot_count - 1].set(NBR - 1)
    return columns.astype(jnp.int32)


def draw_live_counts(key, part):
    subkeys = jax.random.split(jax.random.fold_in(key, 53), 3)
    counts = jax.random.randint(subkeys[0], (NBR, N_ROW), 1, KT + 1)
    full_segment = jax.random.randint(subkeys[1], (NBR,), 0, N_ROW)
    segment = jnp.arange(N_ROW, dtype=jnp.int32)[None, :]
    counts = jnp.where(segment == full_segment[:, None], KT, counts)
    single_row = jax.random.randint(subkeys[2], (), 0, NBR)
    counts = counts.at[single_row, (full_segment[single_row] + 1) % N_ROW].set(1)
    return counts.astype(jnp.int32)


def setup_inputs(seed: int = 0) -> dict:
    key_of = jax.random.split(jax.random.key(seed), 6)
    block_vecs = draw_block_vecs(jax.random.fold_in(key_of[5], 71), 0)
    direction = draw_direction(jax.random.fold_in(key_of[5], 71), 0)
    blocks = draw_blocks(jax.random.fold_in(key_of[5], 71), 0)
    block_cols = draw_block_cols(jax.random.fold_in(key_of[5], 71), 0)
    live_counts = draw_live_counts(jax.random.fold_in(key_of[5], 71), 0)
    return dict(block_vecs=block_vecs, direction=direction, blocks=blocks, block_cols=block_cols, live_counts=live_counts)


highest = lax.Precision.HIGHEST

def outer(left, right):
    return jnp.dot(left.astype(jnp.float32), right.T.astype(jnp.float32), precision=highest, preferred_element_type=jnp.float32)

def apply_matrix(vectors, blocks, block_cols, live_counts):
    vec_width = vectors.shape[0]
    block_rows = blocks.shape[0]
    slot_count = blocks.shape[1]
    block_size = blocks.shape[2]
    source = vectors.reshape(vec_width, block_rows, block_size)
    live_mask = ((jnp.arange(slot_count, dtype=jnp.int32) % KT)[None, :] < jnp.repeat(live_counts, KT, axis=1)).astype(jnp.float32)

    def one_slot(slot, carry):
        forward, backward = carry
        block_tile = lax.dynamic_index_in_dim(blocks, slot, 1, keepdims=False).astype(jnp.float32)
        target = lax.dynamic_index_in_dim(block_cols, slot, 1, keepdims=False)
        weight = lax.dynamic_index_in_dim(live_mask, slot, 1, keepdims=False)
        picked = source[:, target, :] * weight[None, :, None]
        forward = forward + jnp.einsum('vbj,bij->vbi', picked, block_tile, precision=highest)
        spread = jnp.einsum('vbi,bij->vbj', source, block_tile, precision=highest) * weight[None, :, None]
        backward = backward.at[:, target, :].add(spread)
        return (forward, backward)
    empty_acc = jnp.zeros((vec_width, block_rows, block_size), jnp.float32)
    forward, backward = lax.fori_loop(0, slot_count, one_slot, (empty_acc, empty_acc))
    return (0.5 * (forward + backward)).reshape(vec_width, -1)

def reference(block_vecs, direction, blocks, block_cols, live_counts):
    paired = jnp.concatenate([block_vecs, direction], axis=0)
    image_pair = apply_matrix(paired, blocks, block_cols, live_counts)
    image_x = image_pair[:W]
    image_p = image_pair[W:]
    gram_x = outer(block_vecs, block_vecs)
    cross_x = outer(block_vecs, image_x)
    factor_x = jnp.linalg.cholesky(gram_x)
    coefficient = jax.scipy.linalg.cho_solve((factor_x, True), cross_x)
    resid = image_x - jnp.dot(coefficient.T.astype(jnp.float32), block_vecs.astype(jnp.float32), precision=highest, preferred_element_type=jnp.float32)
    image_r = apply_matrix(resid, blocks, block_cols, live_counts)
    basis = jnp.concatenate([block_vecs, resid, direction], axis=0)
    basis_image = jnp.concatenate([image_x, image_r, image_p], axis=0)
    gram_basis = outer(basis, basis)
    gram_apply = outer(basis, basis_image)
    factor = jnp.linalg.cholesky(gram_basis)
    halfway = jax.scipy.linalg.solve_triangular(factor, 0.5 * (gram_apply + gram_apply.T), lower=True)
    reduced = jax.scipy.linalg.solve_triangular(factor, halfway.T, lower=True)
    shifted = reduced + 3.0 * jnp.eye(3 * W, dtype=jnp.float32)
    target = jnp.dot(shifted.astype(jnp.float32), shifted[:, :W].astype(jnp.float32), precision=highest, preferred_element_type=jnp.float32)
    mixing = jax.scipy.linalg.solve_triangular(factor.T, target, lower=False)
    fresh = jnp.dot(mixing.T.astype(jnp.float32), basis.astype(jnp.float32), precision=highest, preferred_element_type=jnp.float32)
    factor_fresh = jnp.linalg.cholesky(outer(fresh, fresh))
    x_next = math.sqrt(ORDER) * jax.scipy.linalg.solve_triangular(factor_fresh, fresh, lower=True)
    return (x_next, reduced, resid)
```

```python
import functools
import math

import jax
import jax.numpy as jnp
from jax import lax
from jax.experimental import pallas as pl
from jax.experimental.pallas import tpu as pltpu
from jax.sharding import PartitionSpec as P

MESH = pl.DeviceIdType.MESH
F32 = jnp.float32
BF16 = jnp.bfloat16
LANES = 128
NT = (((1,), (1,)), ((), ()))
NN = (((1,), (0,)), ((), ()))

AG1_ROW, AG1_COL, RS1_ROW, RS1_COL = 0, 1, 2, 3
AG2_ROW, AG2_COL, RS2_ROW, RS2_COL = 4, 5, 6, 7
AR1_ROW, AR1_COL, AR2_ROW, AR2_COL, AR3_ROW, AR3_COL = 8, 9, 10, 11, 12, 13
STAGES = 14


def mm(left, right, dims=NN):
    return lax.dot_general(
        left, right, dims, precision=lax.Precision.HIGHEST, preferred_element_type=F32
    )


def fast_mm(left, right, dims=NN):
    return lax.dot_general(left, right, dims, preferred_element_type=F32)


def split_rows(value):
    high = value.astype(BF16)
    low = (value - high.astype(F32)).astype(BF16)
    return jnp.concatenate([high, low], axis=0)


def pad_rows(value, rows):
    return jnp.concatenate(
        [value, jnp.zeros((rows - value.shape[0], value.shape[1]), value.dtype)], axis=0
    )


def lanes_of(rows):
    return lax.broadcasted_iota(jnp.int32, (rows, LANES), 1)


def subs_of(rows):
    return lax.broadcasted_iota(jnp.int32, (rows, LANES), 0)


def eliminate(work, order):
    lane, sub = lanes_of(order), subs_of(order)

    def step(k, work):
        row = jnp.sum(jnp.where(sub == k, work, 0.0), axis=0, keepdims=True)
        col = jnp.sum(jnp.where(lane == k, work, 0.0), axis=1, keepdims=True)
        pivot = jnp.sum(jnp.where(lane[:1] == k, row, 0.0), axis=1, keepdims=True)
        inverse = 1.0 / jnp.sqrt(pivot)
        row = row * inverse
        col = col * inverse
        return jnp.where(sub == k, row, jnp.where(sub > k, work - col * row, work))

    return lax.fori_loop(0, order, step, work)


def step_kernel(
    n_row,
    n_col,
    x_ref,
    p_ref,
    blocks_hbm,
    cols_s,
    live_s,
    cols_v,
    live_v,
    next_ref,
    reduced_ref,
    resid_ref,
    blk,
    rp1,
    cp1,
    g1,
    fs1,
    bs1,
    fr1,
    br1,
    rp2,
    cp2,
    g2,
    fs2,
    bs2,
    fr2,
    br2,
    ar1r,
    ar1c,
    ar2r,
    ar2c,
    ar3r,
    ar3c,
    send_sem,
    recv_sem,
    blk_sem,
):
    me_r = lax.axis_index("row")
    me_c = lax.axis_index("col")
    width, span = x_ref.shape
    per = span // LANES
    nb = blocks_hbm.shape[0]
    ncb = per * n_col
    slots = 2 * nb
    order_total = span * n_row * n_col
    sizes = {"row": n_row, "col": n_col}
    mine = {"row": me_r, "col": me_c}

    def copy_to(axis, stage, src, dst, peer):
        return pltpu.make_async_remote_copy(
            src_ref=src,
            dst_ref=dst,
            send_sem=send_sem.at[stage, peer],
            recv_sem=recv_sem.at[stage, mine[axis]],
            device_id={axis: peer},
            device_id_type=MESH,
        )

    def arrival(axis, stage, dst, source):
        return pltpu.make_async_remote_copy(
            src_ref=dst,
            dst_ref=dst,
            send_sem=send_sem.at[stage, source],
            recv_sem=recv_sem.at[stage, source],
            device_id={axis: source},
            device_id_type=MESH,
        )

    def over_peers(axis, body, carry=0):
        n = sizes[axis]
        return lax.fori_loop(
            1, n, lambda d, c: body(lax.rem(mine[axis] + d, n), c), carry
        )

    def share(axis, stage, buf):
        own = buf.at[mine[axis]]

        def body(peer, c):
            copy_to(axis, stage, own, own, peer).start()
            return c

        over_peers(axis, body)

    def collect(axis, stage, buf):
        def body(source, c):
            arrival(axis, stage, buf.at[source], source).wait_recv()
            return c

        over_peers(axis, body)

    def drain(axis, stage, buf):
        def body(peer, c):
            copy_to(axis, stage, buf.at[mine[axis]], buf.at[mine[axis]], peer).wait_send()
            return c

        over_peers(axis, body)

    def total_of(buf, n):
        return lax.fori_loop(1, n, lambda i, t: t + buf[i], buf[0])

    def sum_begin(axis, stage, buf, value):
        buf[mine[axis]] = value
        share(axis, stage, buf)

    def sum_end(axis, stage, buf):
        collect(axis, stage, buf)
        return total_of(buf, sizes[axis])

    fetch = pltpu.make_async_copy(blocks_hbm, blk, blk_sem)
    fetch.start()
    barrier = pltpu.get_barrier_semaphore()
    for axis in ("row", "col"):

        def greet(peer, c, axis=axis):
            pl.semaphore_signal(
                barrier, inc=1, device_id={axis: peer}, device_id_type=MESH
            )
            return c

        over_peers(axis, greet)

    x_now = x_ref[...]
    p_now = p_ref[...]
    for o in range(per):
        piece = jnp.concatenate(
            [x_now[:, o * LANES : (o + 1) * LANES], p_now[:, o * LANES : (o + 1) * LANES]],
            axis=0,
        )
        rp1[me_r, o] = piece
        cp1[me_c, o] = piece
    pl.semaphore_wait(barrier, n_row + n_col - 2)

    share("col", AG1_COL, cp1)
    share("row", AG1_ROW, rp1)

    row_step = per * n_row
    hot = []
    for k in range(2):
        cols = cols_v[:, k : k + 1]
        place = cols // row_step * per + cols % per
        weight = jnp.where(live_v[...] > k, 0.5, 0.0)
        hot.append(
            jnp.where(lax.broadcasted_iota(jnp.int32, (nb, LANES), 1) == place, weight, 0.0)
        )
    hot = jnp.concatenate(hot, axis=0)
    if slots < LANES:
        hot = pad_rows(hot, LANES)
    hot = hot.T[:ncb, :slots].astype(BF16)
    hot = jnp.concatenate([hot, hot], axis=1)

    def pair_of(b):
        return jnp.concatenate([blk[b, 0], blk[b, 1]], axis=1)

    def backward(panel, prod, spread, v):
        def group(r, c):
            for o in range(per):
                b = r * per + o
                out = fast_mm(split_rows(panel[r, o]), pair_of(b))
                out = out[:v] + out[v:]
                for k in range(2):
                    start = pl.multiple_of((k * nb + b) * v, v)
                    prod[pl.ds(start, v), :] = out[:, k * LANES : (k + 1) * LANES]
            return c

        lax.fori_loop(0, n_row, group, 0)
        for vec in range(v):
            part = split_rows(prod[pl.ds(vec, slots, stride=v), :])
            spread[pl.ds(vec, ncb, stride=v), :] = fast_mm(hot, part)

    def spread_piece(spread, v, c):
        return spread.at[pl.ds(pl.multiple_of(c * per * v, per * v), per * v), :]

    def send_back(stage, spread, landed, v):
        def body(peer, c):
            copy_to("col", stage, spread_piece(spread, v, peer), landed.at[me_c], peer).start()
            return c

        over_peers("col", body)

    def forward_group(panel, out_buf, v, r):
        for o in range(per):
            b = r * per + o
            picked = []
            for k in range(2):
                g = cols_s[b, k]
                weight = jnp.where(live_s[b, 0] > k, 0.5, 0.0)
                picked.append(panel[g // row_step, g % per] * weight)
            out = fast_mm(split_rows(jnp.concatenate(picked, axis=1)), pair_of(b), NT)
            start = o * v
            out_buf[r, start : start + v, :] = out[:v] + out[v:]

    def forward(stage, panel, out_buf, landed, v):
        def body(peer, c):
            forward_group(panel, out_buf, v, peer)
            copy_to("row", stage, out_buf.at[peer], landed.at[me_r], peer).start()
            return c

        over_peers("row", body)
        forward_group(panel, out_buf, v, me_r)

    def gather_sum(stage_row, stage_col, fs, bs, fr, br, v):
        start = pl.multiple_of(me_c * per * v, per * v)
        total = fs[me_r] + bs[pl.ds(start, per * v), :]

        def row_body(source, t):
            arrival("row", stage_row, fr.at[source], source).wait_recv()
            return t + fr[source]

        total = over_peers("row", row_body, total)

        def col_body(source, t):
            arrival("col", stage_col, br.at[source], source).wait_recv()
            return t + br[source]

        return over_peers("col", col_body, total)

    def drain_apply(stage_row, stage_col, fs, bs, fr, br, v):
        def row_body(peer, c):
            copy_to("row", stage_row, fs.at[peer], fr.at[me_r], peer).wait_send()
            return c

        over_peers("row", row_body)

        def col_body(peer, c):
            copy_to("col", stage_col, spread_piece(bs, v, peer), br.at[me_c], peer).wait_send()
            return c

        over_peers("col", col_body)

    v1, v2 = 2 * width, width
    fetch.wait()
    collect("row", AG1_ROW, rp1)
    backward(rp1, g1, bs1, v1)
    send_back(RS1_COL, bs1, br1, v1)
    collect("col", AG1_COL, cp1)
    forward(RS1_ROW, cp1, fs1, fr1, v1)
    image = gather_sum(RS1_ROW, RS1_COL, fs1, bs1, fr1, br1, v1)

    image_x, image_p = [], []
    for o in range(per):
        top = image[o * v1 : o * v1 + width]
        image_x.append(top)
        image_p.append(image[o * v1 + width : (o + 1) * v1])
        rp2[me_r, o] = top
        cp2[me_c, o] = top
    share("col", AG2_COL, cp2)
    share("row", AG2_ROW, rp2)
    image_x = jnp.concatenate(image_x, axis=1)
    image_p = jnp.concatenate(image_p, axis=1)

    gap = jnp.zeros((width, span), F32)
    right = jnp.concatenate([x_now, gap, p_now, gap, image_x, gap, image_p, gap], axis=0)
    sum_begin("row", AR1_ROW, ar1r, mm(jnp.concatenate([x_now, p_now], axis=0), right, NT))

    collect("row", AG2_ROW, rp2)
    backward(rp2, g2, bs2, v2)
    send_back(RS2_COL, bs2, br2, v2)
    sum_begin("col", AR1_COL, ar1c, sum_end("row", AR1_ROW, ar1r))
    collect("col", AG2_COL, cp2)
    forward(RS2_ROW, cp2, fs2, fr2, v2)

    first = sum_end("col", AR1_COL, ar1c)
    row_x, row_p = first[:width], first[width:]
    lane, sub = lanes_of(width), subs_of(width)
    work = jnp.where((lane < width) | ((lane >= 64) & (lane < 64 + width)), row_x, 0.0)
    work = eliminate(work + jnp.where(lane == sub + 96, 1.0, 0.0), width)
    halfway = jnp.where(lane < width, pltpu.roll(work, 64, 1), 0.0)
    inverse = jnp.where(lane < width, pltpu.roll(work, 32, 1), 0.0)
    coef_t = mm(pad_rows(halfway, LANES).T[:width], pad_rows(inverse, LANES))
    moved = mm(coef_t, pad_rows(jnp.concatenate([x_now, image_x], axis=1), LANES))
    resid = image_x - moved[:, :span]
    resid_ref[...] = resid

    right = jnp.concatenate([x_now, resid, p_now, gap, image_x, gap, image_p, gap], axis=0)
    sum_begin("row", AR2_ROW, ar2r, mm(resid, right, NT))
    sum_begin("col", AR2_COL, ar2c, sum_end("row", AR2_ROW, ar2r))

    again = gather_sum(RS2_ROW, RS2_COL, fs2, bs2, fr2, br2, v2)
    again = jnp.concatenate([again[o * v2 : (o + 1) * v2] for o in range(per)], axis=1)
    image_r = again - moved[:, span:]
    sum_begin("row", AR3_ROW, ar3r, mm(image_r, right, NT))
    row_r = sum_end("col", AR2_COL, ar2c)
    sum_begin("col", AR3_COL, ar3c, sum_end("row", AR3_ROW, ar3r))

    full = 3 * width
    lane, sub = lanes_of(full), subs_of(full)
    rows = jnp.concatenate([row_x, row_r, row_p], axis=0)
    middle = (lane >= width) & (lane < 2 * width)
    outside = (sub < width) | (sub >= 2 * width)
    flipped = pad_rows(rows, LANES).T[:full]
    gram = jnp.where(lane < full, jnp.where(middle & outside, flipped, rows), 0.0)
    work = eliminate(gram + jnp.where(lane == sub + 64, 1.0, 0.0), full)
    inverse = jnp.where(lane < full, pltpu.roll(work, 64, 1), 0.0)
    inverse_pad = pad_rows(inverse, LANES)
    known = jnp.where((lane < full) & jnp.logical_not(middle), pltpu.roll(rows, 64, 1), 0.0)
    known = 0.5 * (known + pad_rows(known, LANES).T[:full])

    last = sum_end("col", AR3_COL, ar3c)
    last = jnp.where(lanes_of(width) < full, last, 0.0)
    edge = jnp.zeros((width, LANES), F32)
    last = jnp.concatenate([edge, last, edge], axis=0)
    middle_matrix = known + 0.5 * (last + pad_rows(last, LANES).T[:full])

    reduced = mm(mm(inverse, pad_rows(middle_matrix, LANES)), inverse_pad, NT)
    reduced_ref[...] = reduced[:, :full]
    shifted = reduced + jnp.where(lane == sub, 3.0, 0.0)
    target_t = mm(shifted[:width], pad_rows(shifted, LANES))
    mixing_t = mm(target_t, inverse_pad)
    gram_new = mm(target_t, pad_rows(target_t, LANES), NT)
    lane = lanes_of(width)
    work = jnp.where(lane < width, gram_new, 0.0) + pltpu.roll(mixing_t, 64, 1)
    work = eliminate(work, width)
    final = jnp.where(lane < full, pltpu.roll(work, 64, 1), 0.0) * math.sqrt(order_total)
    next_ref[...] = mm(final, pad_rows(jnp.concatenate([x_now, resid, p_now], axis=0), LANES))

    drain("row", AG1_ROW, rp1)
    drain("col", AG1_COL, cp1)
    drain("row", AG2_ROW, rp2)
    drain("col", AG2_COL, cp2)
    drain("row", AR1_ROW, ar1r)
    drain("col", AR1_COL, ar1c)
    drain("row", AR2_ROW, ar2r)
    drain("col", AR2_COL, ar2c)
    drain("row", AR3_ROW, ar3r)
    drain("col", AR3_COL, ar3c)
    drain_apply(RS1_ROW, RS1_COL, fs1, bs1, fr1, br1, v1)
    drain_apply(RS2_ROW, RS2_COL, fs2, bs2, fr2, br2, v2)


def per_device(block_vecs, direction, blocks, block_cols, live_counts):
    n_row = lax.axis_size("row")
    n_col = lax.axis_size("col")
    width, span = block_vecs.shape
    per = span // LANES
    nb = blocks.shape[0]
    v1, v2 = 2 * width, width
    vmem = pl.BlockSpec(memory_space=pltpu.VMEM)
    smem = pl.BlockSpec(memory_space=pltpu.SMEM)

    def panels(v):
        return [
            pltpu.VMEM((n_row, per, v, LANES), F32),
            pltpu.VMEM((n_col, per, v, LANES), F32),
            pltpu.VMEM((2 * nb * v, LANES), F32),
            pltpu.VMEM((n_row, per * v, LANES), F32),
            pltpu.VMEM((n_col * per * v, LANES), F32),
            pltpu.VMEM((n_row, per * v, LANES), F32),
            pltpu.VMEM((n_col, per * v, LANES), F32),
        ]

    sums = []
    for rows in (2 * width, width, width):
        sums += [pltpu.VMEM((n_row, rows, LANES), F32), pltpu.VMEM((n_col, rows, LANES), F32)]
    peers = max(n_row, n_col)
    return pl.pallas_call(
        functools.partial(step_kernel, n_row, n_col),
        out_shape=(
            jax.ShapeDtypeStruct((width, span), F32),
            jax.ShapeDtypeStruct((3 * width, 3 * width), F32),
            jax.ShapeDtypeStruct((width, span), F32),
        ),
        in_specs=[
            vmem,
            vmem,
            pl.BlockSpec(memory_space=pl.ANY),
            smem,
            smem,
            vmem,
            vmem,
        ],
        out_specs=(vmem, vmem, vmem),
        scratch_shapes=[
            pltpu.VMEM(blocks.shape, blocks.dtype),
            *panels(v1),
            *panels(v2),
            *sums,
            pltpu.SemaphoreType.DMA((STAGES, peers)),
            pltpu.SemaphoreType.DMA((STAGES, peers)),
            pltpu.SemaphoreType.DMA(()),
        ],
        compiler_params=pltpu.CompilerParams(
            collective_id=0, has_side_effects=True, vmem_limit_bytes=48 * 2**20
        ),
    )(block_vecs, direction, blocks, block_cols, live_counts, block_cols, live_counts)


def solution(mesh):
    return jax.shard_map(
        per_device,
        mesh=mesh,
        in_specs=(
            P(None, ("col", "row")),
            P(None, ("col", "row")),
            P("col", "row", None, None),
            P("col", "row"),
            P("col", "row"),
        ),
        out_specs=(P(None, ("col", "row")), P(), P(None, ("col", "row"))),
        check_vma=False,
    )
```

```python
import functools
import math

import jax
import jax.numpy as jnp
from jax import lax
from jax.experimental import pallas as pl
from jax.experimental.pallas import tpu as pltpu
from jax.sharding import PartitionSpec as P

MESH = pl.DeviceIdType.MESH
F32 = jnp.float32
BF16 = jnp.bfloat16
LANES = 128
NT = (((1,), (1,)), ((), ()))
NN = (((1,), (0,)), ((), ()))

AGX_ROW, AGX_COL, AGP_ROW, AGP_COL, AGR_ROW, AGR_COL, RS_ROW, RS_COL = range(0, 16, 2)
AR1, AR2, AR3 = 16, 19, 22
STAGES = 25


def mm(left, right, dims=NN):
    return lax.dot_general(
        left, right, dims, precision=lax.Precision.HIGHEST, preferred_element_type=F32
    )


def fast_mm(left, right, dims=NN):
    return lax.dot_general(left, right, dims, preferred_element_type=F32)


def split_rows(value):
    high = value.astype(BF16)
    low = (value - high.astype(F32)).astype(BF16)
    return jnp.concatenate([high, low], axis=0)


def pad_rows(value, rows):
    return jnp.concatenate(
        [value, jnp.zeros((rows - value.shape[0], value.shape[1]), value.dtype)], axis=0
    )


def lanes_of(rows):
    return lax.broadcasted_iota(jnp.int32, (rows, LANES), 1)


def subs_of(rows):
    return lax.broadcasted_iota(jnp.int32, (rows, LANES), 0)


def eliminate(work, begin, end):
    rows = work.shape[0]
    lane, sub = lanes_of(rows), subs_of(rows)

    def step(k, work):
        row = jnp.sum(jnp.where(sub == k, work, 0.0), axis=0, keepdims=True)
        col = jnp.sum(jnp.where(lane == k, work, 0.0), axis=1, keepdims=True)
        pivot = jnp.sum(jnp.where(lane[:1] == k, row, 0.0), axis=1, keepdims=True)
        inverse = 1.0 / jnp.sqrt(pivot)
        row = row * inverse
        col = col * inverse
        return jnp.where(sub == k, row, jnp.where(sub > k, work - col * row, work))

    return lax.fori_loop(begin, end, step, work)


def symmetric(value):
    return value + pad_rows(value, LANES).T[: value.shape[0]]


def band(value, start, stop, shift=0):
    lane = lanes_of(value.shape[0])
    kept = jnp.where((lane >= start) & (lane < stop), value, 0.0)
    return pltpu.roll(kept, shift % LANES, 1) if shift % LANES else kept


def step_kernel(
    n_row,
    n_col,
    x_hbm,
    p_hbm,
    blocks_hbm,
    cols_s,
    live_s,
    cols_v,
    live_v,
    next_ref,
    reduced_ref,
    resid_ref,
    blk,
    x_ref,
    p_ref,
    rpx,
    cpx,
    rpp,
    cpp,
    rpr,
    cpr,
    prod,
    spread,
    fs,
    fp,
    ra_row,
    rb_row,
    ra_col,
    rb_col,
    sum_row,
    sum_col,
    sum_quad,
    send_sem,
    recv_sem,
    fetch_sem,
):
    me = {"row": lax.axis_index("row"), "col": lax.axis_index("col")}
    sizes = {"row": n_row, "col": n_col}
    me_r, me_c = me["row"], me["col"]
    twin = {axis: me[axis] + 1 - 2 * lax.rem(me[axis], 2) for axis in me}
    width, span = x_hbm.shape
    per = span // LANES
    nb = blocks_hbm.shape[0]
    ncb = per * n_col
    slots = 2 * nb
    order_total = span * n_row * n_col
    pending = []

    def copy_to(axis, stage, mark, src, dst, peer):
        return pltpu.make_async_remote_copy(
            src_ref=src,
            dst_ref=dst,
            send_sem=send_sem.at[stage, mark[0]],
            recv_sem=recv_sem.at[stage, mark[1]],
            device_id=peer if isinstance(peer, dict) else {axis: peer},
            device_id_type=MESH,
        )

    def alike(axis, first, body, carry=0, base=None):
        n = sizes[axis]
        base = me[axis] if base is None else base
        return lax.fori_loop(
            first, n // 2, lambda d, c: body(lax.rem(base + 2 * d, n), c), carry
        )

    def plain(body):
        def run(i, c):
            body(i)
            return c

        return run

    def gather_begin(axis, stage, buf):
        own = buf.at[me[axis]]

        def to_peer(peer):
            return copy_to(axis, stage, (peer, me[axis]), own, own, peer)

        alike(axis, 1, plain(lambda peer: to_peer(peer).start()))
        to_peer(twin[axis]).start()
        pending.append(lambda: alike(axis, 1, plain(lambda peer: to_peer(peer).wait_send())))
        pending.append(lambda: to_peer(twin[axis]).wait_send())

    def gather_relay(axis, stage, buf):
        def onward(slot):
            part = buf.at[slot]
            return copy_to(axis, stage + 1, (slot, slot), part, part, twin[axis])

        def relay(source):
            part = buf.at[source]
            copy_to(axis, stage, (source, source), part, part, source).wait_recv()
            onward(source).start()

        alike(axis, 1, plain(relay))
        pending.append(lambda: alike(axis, 1, plain(lambda slot: onward(slot).wait_send())))

    def gather_finish(axis, stage, buf):
        def landed(slot):
            part = buf.at[slot]
            copy_to(axis, stage + 1, (slot, slot), part, part, twin[axis]).wait_recv()

        other = twin[axis]
        part = buf.at[other]
        copy_to(axis, stage, (other, other), part, part, other).wait_recv()
        alike(axis, 1, plain(landed), base=other)

    def scatter_begin(axis, stage, piece, first):
        def to_twin(dest):
            return copy_to(
                axis, stage, (dest, dest), piece(dest), first.at[dest // 2], twin[axis]
            )

        alike(axis, 0, plain(lambda dest: to_twin(dest).start()), base=twin[axis])
        pending.append(
            lambda: alike(axis, 0, plain(lambda dest: to_twin(dest).wait_send()), base=twin[axis])
        )

    def from_twin(axis, stage, piece, first, dest):
        copy_to(
            axis, stage, (dest, dest), piece(dest), first.at[dest // 2], twin[axis]
        ).wait_recv()
        return piece(dest)[...] + first[dest // 2]

    def scatter_relay(axis, stage, piece, first, second):
        def to_owner(dest):
            return copy_to(
                axis, stage + 1, (dest, me[axis]), piece(dest), second.at[me[axis] // 2], dest
            )

        def relay(dest):
            piece(dest)[...] = from_twin(axis, stage, piece, first, dest)
            to_owner(dest).start()

        alike(axis, 1, plain(relay))
        pending.append(lambda: alike(axis, 1, plain(lambda dest: to_owner(dest).wait_send())))

    def scatter_finish(axis, stage, piece, first, second):
        total = from_twin(axis, stage, piece, first, me[axis])

        def add(source, total):
            part = second.at[source // 2]
            copy_to(axis, stage + 1, (source, source), part, part, source).wait_recv()
            return total + second[source // 2]

        return alike(axis, 1, add, total)

    quad = 2 * lax.rem(me_r, 2) + lax.rem(me_c, 2)

    def others():
        for dr, dc in ((1, 0), (0, 1), (1, 1)):
            row = twin["row"] if dr else me_r
            col = twin["col"] if dc else me_c
            yield {"row": row, "col": col}, 2 * lax.rem(row, 2) + lax.rem(col, 2)

    def sum_axis_begin(axis, stage, buf, value):
        own = buf.at[me[axis] // 2]
        own[...] = value

        def to_peer(peer):
            return copy_to(axis, stage, (peer, me[axis]), own, own, peer)

        alike(axis, 1, plain(lambda peer: to_peer(peer).start()))
        pending.append(lambda: alike(axis, 1, plain(lambda peer: to_peer(peer).wait_send())))

    def sum_axis_end(axis, stage, buf):
        def landed(source):
            part = buf.at[source // 2]
            copy_to(axis, stage, (source, source), part, part, source).wait_recv()

        alike(axis, 1, plain(landed))
        total = buf[0]
        for i in range(1, sizes[axis] // 2):
            total = total + buf[i]
        return total

    def sum_begin(which, base, value):
        sum_axis_begin("row", base, sum_row.at[which], value)

    def sum_second(which, base):
        total = sum_axis_end("row", base, sum_row.at[which])
        sum_axis_begin("col", base + 1, sum_col.at[which], total)

    def sum_third(which, base):
        buf = sum_quad.at[which]
        own = buf.at[quad]
        own[...] = sum_axis_end("col", base + 1, sum_col.at[which])
        for peer, place in others():
            copy = copy_to(None, base + 2, (place, quad), own, own, peer)
            copy.start()
            pending.append(copy.wait_send)

    def sum_end(which, base):
        buf = sum_quad.at[which]
        for peer, place in others():
            part = buf.at[place]
            copy_to(None, base + 2, (place, place), part, part, peer).wait_recv()
        return (buf[0] + buf[1]) + (buf[2] + buf[3])

    fetch = pltpu.make_async_copy(blocks_hbm, blk, fetch_sem.at[0])
    fetch_x = pltpu.make_async_copy(x_hbm, x_ref, fetch_sem.at[1])
    fetch_p = pltpu.make_async_copy(p_hbm, p_ref, fetch_sem.at[2])
    fetch_x.start()
    fetch_p.start()
    barrier = pltpu.get_barrier_semaphore()

    def greet(peer):
        pl.semaphore_signal(barrier, inc=1, device_id=peer, device_id_type=MESH)

    for axis in ("row", "col"):
        alike(axis, 1, plain(lambda peer, axis=axis: greet({axis: peer})))
    for peer, _ in others():
        greet(peer)
    fetch.start()

    fetch_x.wait()
    fetch_p.wait()
    x_now = x_ref[...]
    p_now = p_ref[...]
    for o in range(per):
        rpx[me_r, o] = x_now[:, o * LANES : (o + 1) * LANES]
        cpx[me_c, o] = x_now[:, o * LANES : (o + 1) * LANES]
        rpp[me_r, o] = p_now[:, o * LANES : (o + 1) * LANES]
        cpp[me_c, o] = p_now[:, o * LANES : (o + 1) * LANES]
    pl.semaphore_wait(barrier, n_row // 2 + n_col // 2 + 1)

    gather_begin("row", AGX_ROW, rpx)
    gather_begin("col", AGX_COL, cpx)
    gather_begin("row", AGP_ROW, rpp)
    gather_begin("col", AGP_COL, cpp)

    row_step = per * n_row
    place = cols_v[...] // row_step * per + cols_v[...] % per
    hot = []
    for k in range(2):
        weight = jnp.where(live_v[...] > k, 0.5, 0.0)
        match = lax.broadcasted_iota(jnp.int32, (ncb, nb), 0) == place[k : k + 1]
        hot.append(jnp.where(match, weight, 0.0))
    hot = jnp.concatenate(hot + hot, axis=1).astype(BF16)
    gap = jnp.zeros((width, span), F32)
    gaps = jnp.zeros((LANES - 4 * width, span), F32)
    gram_x = mm(x_now, jnp.concatenate([x_now, gap, p_now, gap, gaps], axis=0), NT)
    gram_p = mm(p_now, jnp.concatenate([gap, gap, gap, p_now, gaps], axis=0), NT)

    def pair_of(b):
        return jnp.concatenate([blk[b, 0], blk[b, 1]], axis=1)

    def flat(panel, r):
        return jnp.concatenate([panel[r, o] for o in range(per)], axis=1)

    def backward(panel):
        def group(r):
            for o in range(per):
                b = r * per + o
                out = fast_mm(split_rows(panel[r, o]), pair_of(b))
                out = out[:width] + out[width:]
                for k in range(2):
                    start = pl.multiple_of((k * nb + b) * width, width)
                    prod[pl.ds(start, width), :] = out[:, k * LANES : (k + 1) * LANES]

        lax.fori_loop(0, n_row, plain(group), 0)
        for vec in range(width):
            part = split_rows(prod[pl.ds(vec, slots, stride=width), :])
            spread[pl.ds(vec, ncb, stride=width), :] = fast_mm(hot, part)

    def forward_group(panel, r):
        outs = []
        for o in range(per):
            b = r * per + o
            picked = []
            for k in range(2):
                g = cols_s[k, b]
                weight = jnp.where(live_s[0, b] > k, 0.5, 0.0)
                picked.append(panel[g // row_step, g % per] * weight)
            out = fast_mm(split_rows(jnp.concatenate(picked, axis=1)), pair_of(b), NT)
            outs.append(out[:width] + out[width:])
        return outs

    def bilinear(left, right):
        high = left.astype(BF16)
        low = (left - high.astype(F32)).astype(BF16)
        rows = jnp.concatenate([high, low], axis=0)
        r_high = right.astype(BF16)
        r_low = (right - r_high.astype(F32)).astype(BF16)
        return fast_mm(
            jnp.concatenate([rows, rows], axis=1), jnp.concatenate([r_high, r_low], axis=1), NT
        )

    def fs_piece(i):
        return fs.at[i]

    def spread_piece(i):
        size = per * width
        return spread.at[pl.ds(pl.multiple_of(i * size, size), size), :]

    gather_relay("row", AGX_ROW, rpx)
    gather_relay("col", AGX_COL, cpx)
    fetch.wait()
    gather_finish("row", AGX_ROW, rpx)
    backward(rpx)
    scatter_begin("col", RS_COL, spread_piece, ra_col)
    gather_finish("col", AGX_COL, cpx)

    def first_group(r, total):
        outs = forward_group(cpx, r)
        for o in range(per):
            fs[r, o * width : (o + 1) * width, :] = outs[o]
        right = jnp.concatenate([gap, jnp.concatenate(outs, axis=1), gap, gap, gaps], axis=0)
        return total + bilinear(flat(rpx, r), right)

    own_xx = lax.fori_loop(0, n_row, first_group, jnp.zeros((2 * width, LANES), F32))
    scatter_begin("row", RS_ROW, fs_piece, ra_row)
    scatter_relay("col", RS_COL, spread_piece, ra_col, rb_col)
    sum_begin(0, AR1, gram_x + gram_p + (own_xx[:width] + own_xx[width:]))
    scatter_relay("row", RS_ROW, fs_piece, ra_row, rb_row)
    sum_second(0, AR1)
    gather_relay("row", AGP_ROW, rpp)
    sum_third(0, AR1)
    gather_relay("col", AGP_COL, cpp)
    row_x = sum_end(0, AR1)

    lane, sub = lanes_of(width), subs_of(width)
    half_xx = band(row_x, width, 2 * width, -width)
    cross = symmetric(half_xx)
    work = band(row_x, 0, width) + pltpu.roll(cross, 64, 1)
    work = eliminate(work + jnp.where(lane == sub + 96, 1.0, 0.0), 0, width)
    halfway = band(work, 64, 64 + width, -64)
    inverse = band(work, 96, 96 + width, -96)
    coef_t = mm(pad_rows(halfway, LANES).T[:width], pad_rows(inverse, LANES))
    moved = mm(coef_t, pad_rows(x_now, LANES))

    image = scatter_finish("row", RS_ROW, fs_piece, ra_row, rb_row)
    image = image + scatter_finish("col", RS_COL, spread_piece, ra_col, rb_col)
    image = jnp.concatenate([image[o * width : (o + 1) * width] for o in range(per)], axis=1)
    resid = image - moved
    for o in range(per):
        rpr[me_r, o] = resid[:, o * LANES : (o + 1) * LANES]
        cpr[me_c, o] = resid[:, o * LANES : (o + 1) * LANES]
    gather_begin("col", AGR_COL, cpr)
    gather_begin("row", AGR_ROW, rpr)
    resid_ref[...] = resid

    gram_r = mm(resid, jnp.concatenate([x_now, resid, p_now, image, gaps], axis=0), NT)
    right = jnp.concatenate([gap, gap, gap, gap, p_now, gaps[width:]], axis=0)
    sum_begin(1, AR2, gram_r + mm(image, right, NT))
    gather_finish("row", AGP_ROW, rpp)
    gather_finish("col", AGP_COL, cpp)

    def second_group(r):
        outs = forward_group(cpp, r)
        fp[r] = jnp.concatenate(outs, axis=1)

    lax.fori_loop(0, n_row, plain(second_group), 0)
    gather_relay("row", AGR_ROW, rpr)
    gather_relay("col", AGR_COL, cpr)
    sum_second(1, AR2)
    gather_finish("row", AGR_ROW, rpr)
    gather_finish("col", AGR_COL, cpr)
    sum_third(1, AR2)

    def third_group(r, total):
        outs = forward_group(cpr, r)
        right = jnp.concatenate([gap, jnp.concatenate(outs, axis=1), fp[r], gap, gaps], axis=0)
        left = jnp.concatenate([flat(rpr, r), flat(rpp, r)], axis=0)
        return total + bilinear(left, right)

    own = lax.fori_loop(0, n_row, third_group, jnp.zeros((4 * width, LANES), F32))
    own = own[: 2 * width] + own[2 * width :]
    sum_begin(2, AR3, own[:width] + pltpu.roll(own[width:], 64, 1))

    full = 3 * width
    row_r = sum_end(1, AR2)
    lane, sub = lanes_of(full), subs_of(full)
    row_p = band(row_x, 3 * width, 4 * width, -width)
    gram = jnp.concatenate(
        [
            0.5 * band(row_x, 0, width) + band(row_x, 2 * width, full),
            band(row_r, 0, width) + 0.5 * band(row_r, width, 2 * width) + band(row_r, 2 * width, full),
            0.5 * row_p,
        ],
        axis=0,
    )
    edge = jnp.zeros((width, LANES), F32)
    known = symmetric(
        jnp.concatenate(
            [half_xx + band(row_r, 64, 64 + width, -32), band(row_r, full, full + width, -full), edge],
            axis=0,
        )
    )
    work = symmetric(gram) + jnp.where(lane == sub + 64, 1.0, 0.0)
    work = eliminate(work, 0, width)
    sum_second(2, AR3)
    work = eliminate(work, width, 2 * width)
    sum_third(2, AR3)
    work = eliminate(work, 2 * width, full)
    inverse = band(work, 64, 64 + full, -64)
    inverse_pad = pad_rows(inverse, LANES)

    last = sum_end(2, AR3)
    late = jnp.concatenate([edge, band(last, 0, full), band(last, 64, 64 + full, -64)], axis=0)
    middle = known + symmetric(late)

    reduced = mm(mm(inverse, pad_rows(middle, LANES)), inverse_pad, NT)
    reduced_ref[...] = reduced[:, :full]
    shifted = reduced + jnp.where(lane == sub, 3.0, 0.0)
    target_t = mm(shifted[:width], pad_rows(shifted, LANES))
    mixing_t = mm(target_t, inverse_pad)
    gram_new = mm(target_t, pad_rows(target_t, LANES), NT)
    work = band(gram_new, 0, width) + pltpu.roll(mixing_t, 64, 1)
    work = eliminate(work, 0, width)
    final = band(work, 64, 64 + full, -64) * math.sqrt(order_total)
    next_ref[...] = mm(final, pad_rows(jnp.concatenate([x_now, resid, p_now], axis=0), LANES))

    for leave in pending:
        leave()


def per_device(block_vecs, direction, blocks, block_cols, live_counts):
    n_row = lax.axis_size("row")
    n_col = lax.axis_size("col")
    width, span = block_vecs.shape
    per = span // LANES
    nb = blocks.shape[0]
    vmem = pl.BlockSpec(memory_space=pltpu.VMEM)
    smem = pl.BlockSpec(memory_space=pltpu.SMEM)
    hbm = pl.BlockSpec(memory_space=pltpu.HBM)
    block_cols, live_counts = block_cols.T, live_counts.T
    row_panel = pltpu.VMEM((n_row, per, width, LANES), F32)
    col_panel = pltpu.VMEM((n_col, per, width, LANES), F32)
    row_half = pltpu.VMEM((n_row // 2, per * width, LANES), F32)
    col_half = pltpu.VMEM((n_col // 2, per * width, LANES), F32)
    peers = max(n_row, n_col)
    return pl.pallas_call(
        functools.partial(step_kernel, n_row, n_col),
        out_shape=(
            jax.ShapeDtypeStruct((width, span), F32),
            jax.ShapeDtypeStruct((3 * width, 3 * width), F32),
            jax.ShapeDtypeStruct((width, span), F32),
        ),
        in_specs=[hbm, hbm, hbm, smem, smem, vmem, vmem],
        out_specs=(vmem, vmem, vmem),
        scratch_shapes=[
            pltpu.VMEM(blocks.shape, blocks.dtype),
            pltpu.VMEM((width, span), F32),
            pltpu.VMEM((width, span), F32),
            *([row_panel, col_panel] * 3),
            pltpu.VMEM((2 * nb * width, LANES), F32),
            pltpu.VMEM((n_col * per * width, LANES), F32),
            pltpu.VMEM((n_row, per * width, LANES), F32),
            pltpu.VMEM((n_row, width, span), F32),
            row_half,
            row_half,
            col_half,
            col_half,
            pltpu.VMEM((3, n_row // 2, width, LANES), F32),
            pltpu.VMEM((3, n_col // 2, width, LANES), F32),
            pltpu.VMEM((3, 4, width, LANES), F32),
            pltpu.SemaphoreType.DMA((STAGES, peers)),
            pltpu.SemaphoreType.DMA((STAGES, peers)),
            pltpu.SemaphoreType.DMA((3,)),
        ],
        compiler_params=pltpu.CompilerParams(
            collective_id=0, has_side_effects=True, vmem_limit_bytes=63 * 2**20
        ),
    )(block_vecs, direction, blocks, block_cols, live_counts, block_cols, live_counts)


def solution(mesh):
    return jax.shard_map(
        per_device,
        mesh=mesh,
        in_specs=(
            P(None, ("col", "row")),
            P(None, ("col", "row")),
            P("col", "row", None, None),
            P("col", "row"),
            P("col", "row"),
        ),
        out_specs=(P(None, ("col", "row")), P(), P(None, ("col", "row"))),
        check_vma=False,
    )
```

```python
import functools
import math

import jax
import jax.numpy as jnp
from jax import lax
from jax.experimental import pallas as pl
from jax.experimental.pallas import tpu as pltpu
from jax.sharding import PartitionSpec as P

MESH = pl.DeviceIdType.MESH
F32 = jnp.float32
BF16 = jnp.bfloat16
LANES = 128
NT = (((1,), (1,)), ((), ()))
NN = (((1,), (0,)), ((), ()))

AGX_ROW, AGX_COL, AGP_ROW, AGP_COL, AGR_ROW, AGR_COL, RS_ROW, RS_COL = range(0, 16, 2)
AR1, AR2, AR3 = 16, 19, 22
STAGES = 25


def mm(left, right, dims=NN):
    return lax.dot_general(
        left, right, dims, precision=lax.Precision.HIGHEST, preferred_element_type=F32
    )


def fast_mm(left, right, dims=NN):
    return lax.dot_general(left, right, dims, preferred_element_type=F32)


def split_rows(value):
    high = value.astype(BF16)
    low = (value - high.astype(F32)).astype(BF16)
    return jnp.concatenate([high, low], axis=0)


def pad_rows(value, rows):
    return jnp.concatenate(
        [value, jnp.zeros((rows - value.shape[0], value.shape[1]), value.dtype)], axis=0
    )


def lanes_of(rows):
    return lax.broadcasted_iota(jnp.int32, (rows, LANES), 1)


def subs_of(rows):
    return lax.broadcasted_iota(jnp.int32, (rows, LANES), 0)


def eliminate(work, begin, end):
    rows = work.shape[0]
    lane, sub = lanes_of(rows), subs_of(rows)

    def step(k, work):
        row = jnp.sum(jnp.where(sub == k, work, 0.0), axis=0, keepdims=True)
        col = jnp.sum(jnp.where(lane == k, work, 0.0), axis=1, keepdims=True)
        pivot = jnp.sum(jnp.where(lane[:1] == k, row, 0.0), axis=1, keepdims=True)
        inverse = 1.0 / jnp.sqrt(pivot)
        row = row * inverse
        col = col * inverse
        return jnp.where(sub == k, row, jnp.where(sub > k, work - col * row, work))

    return lax.fori_loop(begin, end, step, work)


def symmetric(value):
    return value + pad_rows(value, LANES).T[: value.shape[0]]


def band(value, start, stop, shift=0):
    lane = lanes_of(value.shape[0])
    kept = jnp.where((lane >= start) & (lane < stop), value, 0.0)
    return pltpu.roll(kept, shift % LANES, 1) if shift % LANES else kept


def step_kernel(
    n_row,
    n_col,
    x_hbm,
    p_hbm,
    blocks_hbm,
    cols_s,
    live_s,
    cols_v,
    live_v,
    next_ref,
    reduced_ref,
    resid_ref,
    blk,
    x_ref,
    p_ref,
    rpx,
    cpx,
    rpp,
    cpp,
    rpr,
    cpr,
    prod,
    spread,
    fs,
    fp,
    ra_row,
    rb_row,
    ra_col,
    rb_col,
    sum_row,
    sum_col,
    sum_quad,
    send_sem,
    recv_sem,
    each_sem,
    fetch_sem,
):
    me = {"row": lax.axis_index("row"), "col": lax.axis_index("col")}
    sizes = {"row": n_row, "col": n_col}
    me_r, me_c = me["row"], me["col"]
    twin = {axis: me[axis] + 1 - 2 * lax.rem(me[axis], 2) for axis in me}
    width, span = x_hbm.shape
    per = span // LANES
    nb = blocks_hbm.shape[0]
    ncb = per * n_col
    slots = 2 * nb
    order_total = span * n_row * n_col
    pending = []

    def copy_to(axis, stage, src, dst, peer, single=None):
        return pltpu.make_async_remote_copy(
            src_ref=src,
            dst_ref=dst,
            send_sem=send_sem.at[stage],
            recv_sem=recv_sem.at[stage] if single is None else each_sem.at[stage // 2, single],
            device_id=peer if isinstance(peer, dict) else {axis: peer},
            device_id_type=MESH,
        )

    def whole(stage, buf, count):
        part = buf.at[pl.ds(0, count)]
        return copy_to("row", stage, part, part, twin["row"])

    def alike(axis, first, body, carry=0, base=None):
        n = sizes[axis]
        base = me[axis] if base is None else base
        return lax.fori_loop(
            first, n // 2, lambda d, c: body(lax.rem(base + 2 * d, n), c), carry
        )

    def plain(body):
        def run(i, c):
            body(i)
            return c

        return run

    def gather_begin(axis, stage, buf):
        own = buf.at[me[axis]]
        half = sizes[axis] // 2
        alike(
            axis,
            1,
            plain(lambda peer: copy_to(axis, stage, own, own, peer, me[axis] // 2).start()),
        )
        copy_to(axis, stage + 1, own, own, twin[axis]).start()
        if half > 1:
            pending.append(lambda: whole(stage, buf, half - 1).wait_send())
        pending.append(lambda: whole(stage + 1, buf, half).wait_send())

    def gather_relay(axis, stage, buf):
        def relay(source):
            part = buf.at[source]
            copy_to(axis, stage, part, part, source, source // 2).wait_recv()
            copy_to(axis, stage + 1, part, part, twin[axis]).start()

        alike(axis, 1, plain(relay))

    def gather_finish(axis, stage, buf):
        whole(stage + 1, buf, sizes[axis] // 2).wait_recv()

    def scatter_begin(axis, stage, piece, first):
        def to_twin(dest):
            copy_to(
                axis, stage, piece(dest), first.at[dest // 2], twin[axis], dest // 2
            ).start()

        alike(axis, 0, plain(to_twin), base=twin[axis])
        pending.append(lambda: whole(stage, first, sizes[axis] // 2).wait_send())

    def from_twin(axis, stage, piece, first, dest):
        part = first.at[dest // 2]
        copy_to(axis, stage, part, part, twin[axis], dest // 2).wait_recv()
        return piece(dest)[...] + first[dest // 2]

    def scatter_relay(axis, stage, piece, first, second):
        def relay(dest):
            piece(dest)[...] = from_twin(axis, stage, piece, first, dest)
            copy_to(axis, stage + 1, piece(dest), second.at[me[axis] // 2], dest).start()

        alike(axis, 1, plain(relay))
        if sizes[axis] > 2:
            pending.append(lambda: whole(stage + 1, second, sizes[axis] // 2 - 1).wait_send())

    def scatter_finish(axis, stage, piece, first, second):
        total = from_twin(axis, stage, piece, first, me[axis])
        if sizes[axis] > 2:
            whole(stage + 1, second, sizes[axis] // 2 - 1).wait_recv()
        return alike(axis, 1, lambda source, total: total + second[source // 2], total)

    quad = 2 * lax.rem(me_r, 2) + lax.rem(me_c, 2)

    def others():
        for dr, dc in ((1, 1), (0, 1), (1, 0)):
            row = twin["row"] if dr else me_r
            col = twin["col"] if dc else me_c
            yield {"row": row, "col": col}

    def sum_axis_begin(axis, stage, buf, value):
        own = buf.at[me[axis] // 2]
        own[...] = value
        alike(axis, 1, plain(lambda peer: copy_to(axis, stage, own, own, peer).start()))
        if sizes[axis] > 2:
            pending.append(lambda: whole(stage, buf, sizes[axis] // 2 - 1).wait_send())

    def sum_axis_end(axis, stage, buf):
        if sizes[axis] > 2:
            whole(stage, buf, sizes[axis] // 2 - 1).wait_recv()
        total = buf[0]
        for i in range(1, sizes[axis] // 2):
            total = total + buf[i]
        return total

    def sum_begin(which, base, value):
        sum_axis_begin("row", base, sum_row.at[which], value)

    def sum_second(which, base):
        total = sum_axis_end("row", base, sum_row.at[which])
        sum_axis_begin("col", base + 1, sum_col.at[which], total)

    def sum_third(which, base):
        buf = sum_quad.at[which]
        own = buf.at[quad]
        own[...] = sum_axis_end("col", base + 1, sum_col.at[which])
        for peer in others():
            copy_to(None, base + 2, own, own, peer).start()
        pending.append(lambda: whole(base + 2, buf, 3).wait_send())

    def sum_end(which, base):
        buf = sum_quad.at[which]
        whole(base + 2, buf, 3).wait_recv()
        return (buf[0] + buf[1]) + (buf[2] + buf[3])

    fetch = pltpu.make_async_copy(blocks_hbm, blk, fetch_sem.at[0])
    fetch_x = pltpu.make_async_copy(x_hbm, x_ref, fetch_sem.at[1])
    fetch_p = pltpu.make_async_copy(p_hbm, p_ref, fetch_sem.at[2])
    fetch_x.start()
    fetch_p.start()
    barrier = pltpu.get_barrier_semaphore()

    def greet(peer):
        pl.semaphore_signal(barrier, inc=1, device_id=peer, device_id_type=MESH)

    for axis in ("row", "col"):
        alike(axis, 1, plain(lambda peer, axis=axis: greet({axis: peer})))
    for peer in others():
        greet(peer)
    fetch.start()

    fetch_x.wait()
    fetch_p.wait()
    x_now = x_ref[...]
    p_now = p_ref[...]
    for o in range(per):
        rpx[me_r, o] = x_now[:, o * LANES : (o + 1) * LANES]
        cpx[me_c, o] = x_now[:, o * LANES : (o + 1) * LANES]
        rpp[me_r, o] = p_now[:, o * LANES : (o + 1) * LANES]
        cpp[me_c, o] = p_now[:, o * LANES : (o + 1) * LANES]
    pl.semaphore_wait(barrier, n_row // 2 + n_col // 2 + 1)

    gather_begin("col", AGX_COL, cpx)
    gather_begin("row", AGX_ROW, rpx)

    row_step = per * n_row
    place = cols_v[...] // row_step * per + cols_v[...] % per
    hot = []
    for k in range(2):
        weight = jnp.where(live_v[...] > k, 0.5, 0.0)
        match = lax.broadcasted_iota(jnp.int32, (ncb, nb), 0) == place[k : k + 1]
        hot.append(jnp.where(match, weight, 0.0))
    hot = jnp.concatenate(hot + hot, axis=1).astype(BF16)
    gap = jnp.zeros((width, span), F32)
    gaps = jnp.zeros((LANES - 4 * width, span), F32)
    gram_x = mm(x_now, jnp.concatenate([x_now, gap, p_now, gap, gaps], axis=0), NT)
    gram_p = mm(p_now, jnp.concatenate([gap, gap, gap, p_now, gaps], axis=0), NT)

    def pair_of(b):
        return jnp.concatenate([blk[b, 0], blk[b, 1]], axis=1)

    def flat(panel, r):
        return jnp.concatenate([panel[r, o] for o in range(per)], axis=1)

    def backward(panel):
        def group(r):
            for o in range(per):
                b = r * per + o
                out = fast_mm(split_rows(panel[r, o]), pair_of(b))
                out = out[:width] + out[width:]
                for k in range(2):
                    start = pl.multiple_of((k * nb + b) * width, width)
                    prod[pl.ds(start, width), :] = out[:, k * LANES : (k + 1) * LANES]

        lax.fori_loop(0, n_row, plain(group), 0)
        for vec in range(width):
            part = split_rows(prod[pl.ds(vec, slots, stride=width), :])
            spread[pl.ds(vec, ncb, stride=width), :] = fast_mm(hot, part)

    def forward_group(panel, r):
        outs = []
        for o in range(per):
            b = r * per + o
            picked = []
            for k in range(2):
                g = cols_s[k, b]
                weight = jnp.where(live_s[0, b] > k, 0.5, 0.0)
                picked.append(panel[g // row_step, g % per] * weight)
            out = fast_mm(split_rows(jnp.concatenate(picked, axis=1)), pair_of(b), NT)
            outs.append(out[:width] + out[width:])
        return outs

    def bilinear(left, right):
        high = left.astype(BF16)
        low = (left - high.astype(F32)).astype(BF16)
        rows = jnp.concatenate([high, low], axis=0)
        r_high = right.astype(BF16)
        r_low = (right - r_high.astype(F32)).astype(BF16)
        return fast_mm(
            jnp.concatenate([rows, rows], axis=1), jnp.concatenate([r_high, r_low], axis=1), NT
        )

    def fs_piece(i):
        return fs.at[i]

    def spread_piece(i):
        size = per * width
        return spread.at[pl.ds(pl.multiple_of(i * size, size), size), :]

    gather_relay("row", AGX_ROW, rpx)
    gather_relay("col", AGX_COL, cpx)
    gather_begin("col", AGP_COL, cpp)
    gather_begin("row", AGP_ROW, rpp)
    fetch.wait()
    gather_finish("row", AGX_ROW, rpx)
    backward(rpx)
    scatter_begin("col", RS_COL, spread_piece, ra_col)
    gather_finish("col", AGX_COL, cpx)

    def first_group(r, total):
        outs = forward_group(cpx, r)
        for o in range(per):
            fs[r, o * width : (o + 1) * width, :] = outs[o]
        right = jnp.concatenate([gap, jnp.concatenate(outs, axis=1), gap, gap, gaps], axis=0)
        return total + bilinear(flat(rpx, r), right)

    own_xx = lax.fori_loop(0, n_row, first_group, jnp.zeros((2 * width, LANES), F32))
    scatter_begin("row", RS_ROW, fs_piece, ra_row)
    scatter_relay("col", RS_COL, spread_piece, ra_col, rb_col)
    sum_begin(0, AR1, gram_x + gram_p + (own_xx[:width] + own_xx[width:]))
    scatter_relay("row", RS_ROW, fs_piece, ra_row, rb_row)
    sum_second(0, AR1)
    gather_relay("row", AGP_ROW, rpp)
    sum_third(0, AR1)
    gather_relay("col", AGP_COL, cpp)
    row_x = sum_end(0, AR1)

    lane, sub = lanes_of(width), subs_of(width)
    half_xx = band(row_x, width, 2 * width, -width)
    cross = symmetric(half_xx)
    work = band(row_x, 0, width) + pltpu.roll(cross, 64, 1)
    work = eliminate(work + jnp.where(lane == sub + 96, 1.0, 0.0), 0, width)
    halfway = band(work, 64, 64 + width, -64)
    inverse = band(work, 96, 96 + width, -96)
    coef_t = mm(pad_rows(halfway, LANES).T[:width], pad_rows(inverse, LANES))
    moved = mm(coef_t, pad_rows(x_now, LANES))

    image = scatter_finish("row", RS_ROW, fs_piece, ra_row, rb_row)
    image = image + scatter_finish("col", RS_COL, spread_piece, ra_col, rb_col)
    image = jnp.concatenate([image[o * width : (o + 1) * width] for o in range(per)], axis=1)
    resid = image - moved
    for o in range(per):
        rpr[me_r, o] = resid[:, o * LANES : (o + 1) * LANES]
        cpr[me_c, o] = resid[:, o * LANES : (o + 1) * LANES]
    gather_begin("col", AGR_COL, cpr)
    gather_begin("row", AGR_ROW, rpr)
    resid_ref[...] = resid

    gram_r = mm(resid, jnp.concatenate([x_now, resid, p_now, image, gaps], axis=0), NT)
    right = jnp.concatenate([gap, gap, gap, gap, p_now, gaps[width:]], axis=0)
    sum_begin(1, AR2, gram_r + mm(image, right, NT))
    gather_finish("row", AGP_ROW, rpp)
    gather_finish("col", AGP_COL, cpp)

    def second_group(r):
        outs = forward_group(cpp, r)
        fp[r] = jnp.concatenate(outs, axis=1)

    lax.fori_loop(0, n_row, plain(second_group), 0)
    gather_relay("row", AGR_ROW, rpr)
    gather_relay("col", AGR_COL, cpr)
    sum_second(1, AR2)
    gather_finish("row", AGR_ROW, rpr)
    gather_finish("col", AGR_COL, cpr)
    sum_third(1, AR2)

    def third_group(r, total):
        outs = forward_group(cpr, r)
        right = jnp.concatenate([gap, jnp.concatenate(outs, axis=1), fp[r], gap, gaps], axis=0)
        left = jnp.concatenate([flat(rpr, r), flat(rpp, r)], axis=0)
        return total + bilinear(left, right)

    own = lax.fori_loop(0, n_row, third_group, jnp.zeros((4 * width, LANES), F32))
    own = own[: 2 * width] + own[2 * width :]
    sum_begin(2, AR3, own[:width] + pltpu.roll(own[width:], 64, 1))

    full = 3 * width
    row_r = sum_end(1, AR2)
    lane, sub = lanes_of(full), subs_of(full)
    row_p = band(row_x, 3 * width, 4 * width, -width)
    gram = jnp.concatenate(
        [
            0.5 * band(row_x, 0, width) + band(row_x, 2 * width, full),
            band(row_r, 0, width) + 0.5 * band(row_r, width, 2 * width) + band(row_r, 2 * width, full),
            0.5 * row_p,
        ],
        axis=0,
    )
    edge = jnp.zeros((width, LANES), F32)
    known = symmetric(
        jnp.concatenate(
            [half_xx + band(row_r, 64, 64 + width, -32), band(row_r, full, full + width, -full), edge],
            axis=0,
        )
    )
    work = symmetric(gram) + jnp.where(lane == sub + 64, 1.0, 0.0)
    work = eliminate(work, 0, width)
    sum_second(2, AR3)
    work = eliminate(work, width, 2 * width)
    sum_third(2, AR3)
    work = eliminate(work, 2 * width, full)
    inverse = band(work, 64, 64 + full, -64)
    inverse_pad = pad_rows(inverse, LANES)

    last = sum_end(2, AR3)
    late = jnp.concatenate([edge, band(last, 0, full), band(last, 64, 64 + full, -64)], axis=0)
    middle = known + symmetric(late)

    reduced = mm(mm(inverse, pad_rows(middle, LANES)), inverse_pad, NT)
    reduced_ref[...] = reduced[:, :full]
    shifted = reduced + jnp.where(lane == sub, 3.0, 0.0)
    target_t = mm(shifted[:width], pad_rows(shifted, LANES))
    mixing_t = mm(target_t, inverse_pad)
    gram_new = mm(target_t, pad_rows(target_t, LANES), NT)
    work = band(gram_new, 0, width) + pltpu.roll(mixing_t, 64, 1)
    work = eliminate(work, 0, width)
    final = band(work, 64, 64 + full, -64) * math.sqrt(order_total)
    next_ref[...] = mm(final, pad_rows(jnp.concatenate([x_now, resid, p_now], axis=0), LANES))

    for leave in pending:
        leave()


def per_device(block_vecs, direction, blocks, block_cols, live_counts):
    n_row = lax.axis_size("row")
    n_col = lax.axis_size("col")
    width, span = block_vecs.shape
    per = span // LANES
    nb = blocks.shape[0]
    vmem = pl.BlockSpec(memory_space=pltpu.VMEM)
    smem = pl.BlockSpec(memory_space=pltpu.SMEM)
    hbm = pl.BlockSpec(memory_space=pltpu.HBM)
    block_cols, live_counts = block_cols.T, live_counts.T
    row_panel = pltpu.VMEM((n_row, per, width, LANES), F32)
    col_panel = pltpu.VMEM((n_col, per, width, LANES), F32)
    row_half = pltpu.VMEM((n_row // 2, per * width, LANES), F32)
    col_half = pltpu.VMEM((n_col // 2, per * width, LANES), F32)
    peers = max(n_row, n_col)
    return pl.pallas_call(
        functools.partial(step_kernel, n_row, n_col),
        out_shape=(
            jax.ShapeDtypeStruct((width, span), F32),
            jax.ShapeDtypeStruct((3 * width, 3 * width), F32),
            jax.ShapeDtypeStruct((width, span), F32),
        ),
        in_specs=[hbm, hbm, hbm, smem, smem, vmem, vmem],
        out_specs=(vmem, vmem, vmem),
        scratch_shapes=[
            pltpu.VMEM(blocks.shape, blocks.dtype),
            pltpu.VMEM((width, span), F32),
            pltpu.VMEM((width, span), F32),
            *([row_panel, col_panel] * 3),
            pltpu.VMEM((2 * nb * width, LANES), F32),
            pltpu.VMEM((n_col * per * width, LANES), F32),
            pltpu.VMEM((n_row, per * width, LANES), F32),
            pltpu.VMEM((n_row, width, span), F32),
            row_half,
            row_half,
            col_half,
            col_half,
            pltpu.VMEM((3, n_row // 2, width, LANES), F32),
            pltpu.VMEM((3, n_col // 2, width, LANES), F32),
            pltpu.VMEM((3, 4, width, LANES), F32),
            pltpu.SemaphoreType.DMA((STAGES,)),
            pltpu.SemaphoreType.DMA((STAGES,)),
            pltpu.SemaphoreType.DMA((8, peers // 2)),
            pltpu.SemaphoreType.DMA((3,)),
        ],
        compiler_params=pltpu.CompilerParams(
            collective_id=0, has_side_effects=True, vmem_limit_bytes=63 * 2**20
        ),
    )(block_vecs, direction, blocks, block_cols, live_counts, block_cols, live_counts)


def solution(mesh):
    return jax.shard_map(
        per_device,
        mesh=mesh,
        in_specs=(
            P(None, ("col", "row")),
            P(None, ("col", "row")),
            P("col", "row", None, None),
            P("col", "row"),
            P("col", "row"),
        ),
        out_specs=(P(None, ("col", "row")), P(), P(None, ("col", "row"))),
        check_vma=False,
    )
```

```python
import functools
import math

import jax
import jax.numpy as jnp
from jax import lax
from jax.experimental import pallas as pl
from jax.experimental.pallas import tpu as pltpu
from jax.sharding import PartitionSpec as P

MESH = pl.DeviceIdType.MESH
F32 = jnp.float32
BF16 = jnp.bfloat16
LANES = 128
NT = (((1,), (1,)), ((), ()))
NN = (((1,), (0,)), ((), ()))

AGX_ROW, AGX_COL, AGP_ROW, AGP_COL, AGR_ROW, AGR_COL, RS_ROW, RS_COL = range(0, 16, 2)
AR1, AR2, AR3 = 16, 19, 22
STAGES = 25


def mm(left, right, dims=NN):
    return lax.dot_general(
        left, right, dims, precision=lax.Precision.HIGHEST, preferred_element_type=F32
    )


def fast_mm(left, right, dims=NN):
    return lax.dot_general(left, right, dims, preferred_element_type=F32)


def split_rows(value):
    high = value.astype(BF16)
    low = (value - high.astype(F32)).astype(BF16)
    return jnp.concatenate([high, low], axis=0)


def pad_rows(value, rows):
    return jnp.concatenate(
        [value, jnp.zeros((rows - value.shape[0], value.shape[1]), value.dtype)], axis=0
    )


def lanes_of(rows):
    return lax.broadcasted_iota(jnp.int32, (rows, LANES), 1)


def subs_of(rows):
    return lax.broadcasted_iota(jnp.int32, (rows, LANES), 0)


def eliminate(work, begin, end):
    rows = work.shape[0]
    lane, sub = lanes_of(rows), subs_of(rows)

    def step(k, work):
        row = jnp.sum(jnp.where(sub == k, work, 0.0), axis=0, keepdims=True)
        col = jnp.sum(jnp.where(lane == k, work, 0.0), axis=1, keepdims=True)
        pivot = jnp.sum(jnp.where(lane[:1] == k, row, 0.0), axis=1, keepdims=True)
        inverse = 1.0 / jnp.sqrt(pivot)
        row = row * inverse
        col = col * inverse
        return jnp.where(sub == k, row, jnp.where(sub > k, work - col * row, work))

    return lax.fori_loop(begin, end, step, work)


def symmetric(value):
    return value + pad_rows(value, LANES).T[: value.shape[0]]


def band(value, start, stop, shift=0):
    lane = lanes_of(value.shape[0])
    kept = jnp.where((lane >= start) & (lane < stop), value, 0.0)
    return pltpu.roll(kept, shift % LANES, 1) if shift % LANES else kept


def step_kernel(
    n_row,
    n_col,
    x_hbm,
    p_hbm,
    blocks_hbm,
    cols_s,
    live_s,
    cols_v,
    live_v,
    next_ref,
    reduced_ref,
    resid_ref,
    blk,
    x_ref,
    p_ref,
    rpx,
    cpx,
    rpp,
    cpp,
    rpr,
    cpr,
    prod,
    spread,
    fs,
    fp,
    ra_row,
    rb_row,
    ra_col,
    rb_col,
    sum_row,
    sum_col,
    sum_quad,
    send_sem,
    recv_sem,
    each_sem,
    fetch_sem,
):
    me = {"row": lax.axis_index("row"), "col": lax.axis_index("col")}
    sizes = {"row": n_row, "col": n_col}
    me_r, me_c = me["row"], me["col"]
    twin = {axis: me[axis] + 1 - 2 * lax.rem(me[axis], 2) for axis in me}
    width, span = x_hbm.shape
    per = span // LANES
    nb = blocks_hbm.shape[0]
    ncb = per * n_col
    slots = 2 * nb
    order_total = span * n_row * n_col
    pending = []

    def copy_to(axis, stage, src, dst, peer, single=None):
        return pltpu.make_async_remote_copy(
            src_ref=src,
            dst_ref=dst,
            send_sem=send_sem.at[stage],
            recv_sem=recv_sem.at[stage] if single is None else each_sem.at[stage // 2, single],
            device_id=peer if isinstance(peer, dict) else {axis: peer},
            device_id_type=MESH,
        )

    def whole(stage, buf, count):
        part = buf.at[pl.ds(0, count)]
        return copy_to("row", stage, part, part, twin["row"])

    def alike(axis, first, body, carry=0, base=None):
        n = sizes[axis]
        base = me[axis] if base is None else base
        for d in sorted(range(first, n // 2), key=lambda d: -min(d, n // 2 - d)):
            carry = body(lax.rem(base + 2 * d, n), carry)
        return carry

    def plain(body):
        def run(i, c):
            body(i)
            return c

        return run

    def gather_begin(axis, stage, buf):
        own = buf.at[me[axis]]
        half = sizes[axis] // 2
        alike(
            axis,
            1,
            plain(lambda peer: copy_to(axis, stage, own, own, peer, me[axis] // 2).start()),
        )
        copy_to(axis, stage + 1, own, own, twin[axis]).start()
        if half > 1:
            pending.append(lambda: whole(stage, buf, half - 1).wait_send())
        pending.append(lambda: whole(stage + 1, buf, half).wait_send())

    def gather_relay(axis, stage, buf):
        def relay(source):
            part = buf.at[source]
            copy_to(axis, stage, part, part, source, source // 2).wait_recv()
            copy_to(axis, stage + 1, part, part, twin[axis]).start()

        alike(axis, 1, plain(relay))

    def gather_finish(axis, stage, buf):
        whole(stage + 1, buf, sizes[axis] // 2).wait_recv()

    def scatter_begin(axis, stage, piece, first):
        def to_twin(dest):
            copy_to(
                axis, stage, piece(dest), first.at[dest // 2], twin[axis], dest // 2
            ).start()

        alike(axis, 0, plain(to_twin), base=twin[axis])
        pending.append(lambda: whole(stage, first, sizes[axis] // 2).wait_send())

    def from_twin(axis, stage, piece, first, dest):
        part = first.at[dest // 2]
        copy_to(axis, stage, part, part, twin[axis], dest // 2).wait_recv()
        return piece(dest)[...] + first[dest // 2]

    def scatter_relay(axis, stage, piece, first, second):
        def relay(dest):
            piece(dest)[...] = from_twin(axis, stage, piece, first, dest)
            copy_to(axis, stage + 1, piece(dest), second.at[me[axis] // 2], dest).start()

        alike(axis, 1, plain(relay))
        if sizes[axis] > 2:
            pending.append(lambda: whole(stage + 1, second, sizes[axis] // 2 - 1).wait_send())

    def scatter_finish(axis, stage, piece, first, second):
        total = from_twin(axis, stage, piece, first, me[axis])
        if sizes[axis] > 2:
            whole(stage + 1, second, sizes[axis] // 2 - 1).wait_recv()
        return alike(axis, 1, lambda source, total: total + second[source // 2], total)

    quad = 2 * lax.rem(me_r, 2) + lax.rem(me_c, 2)

    def others():
        for dr, dc in ((1, 1), (0, 1), (1, 0)):
            row = twin["row"] if dr else me_r
            col = twin["col"] if dc else me_c
            yield {"row": row, "col": col}

    def sum_axis_begin(axis, stage, buf, value):
        own = buf.at[me[axis] // 2]
        own[...] = value
        alike(axis, 1, plain(lambda peer: copy_to(axis, stage, own, own, peer).start()))
        if sizes[axis] > 2:
            pending.append(lambda: whole(stage, buf, sizes[axis] // 2 - 1).wait_send())

    def sum_axis_end(axis, stage, buf):
        if sizes[axis] > 2:
            whole(stage, buf, sizes[axis] // 2 - 1).wait_recv()
        total = buf[0]
        for i in range(1, sizes[axis] // 2):
            total = total + buf[i]
        return total

    def sum_begin(which, base, value):
        sum_axis_begin("row", base, sum_row.at[which], value)

    def sum_second(which, base):
        total = sum_axis_end("row", base, sum_row.at[which])
        sum_axis_begin("col", base + 1, sum_col.at[which], total)

    def sum_third(which, base):
        buf = sum_quad.at[which]
        own = buf.at[quad]
        own[...] = sum_axis_end("col", base + 1, sum_col.at[which])
        for peer in others():
            copy_to(None, base + 2, own, own, peer).start()
        pending.append(lambda: whole(base + 2, buf, 3).wait_send())

    def sum_end(which, base):
        buf = sum_quad.at[which]
        whole(base + 2, buf, 3).wait_recv()
        return (buf[0] + buf[1]) + (buf[2] + buf[3])

    fetch = pltpu.make_async_copy(blocks_hbm, blk, fetch_sem.at[0])
    fetch_x = pltpu.make_async_copy(x_hbm, x_ref, fetch_sem.at[1])
    fetch_p = pltpu.make_async_copy(p_hbm, p_ref, fetch_sem.at[2])
    fetch_x.start()
    fetch_p.start()
    barrier = pltpu.get_barrier_semaphore()

    def greet(peer):
        pl.semaphore_signal(barrier, inc=1, device_id=peer, device_id_type=MESH)

    for axis in ("row", "col"):
        alike(axis, 1, plain(lambda peer, axis=axis: greet({axis: peer})))
    for peer in others():
        greet(peer)
    fetch.start()

    fetch_x.wait()
    fetch_p.wait()
    x_now = x_ref[...]
    p_now = p_ref[...]
    for o in range(per):
        rpx[me_r, o] = x_now[:, o * LANES : (o + 1) * LANES]
        cpx[me_c, o] = x_now[:, o * LANES : (o + 1) * LANES]
        rpp[me_r, o] = p_now[:, o * LANES : (o + 1) * LANES]
        cpp[me_c, o] = p_now[:, o * LANES : (o + 1) * LANES]
    pl.semaphore_wait(barrier, n_row // 2 + n_col // 2 + 1)

    gather_begin("col", AGX_COL, cpx)
    gather_begin("row", AGX_ROW, rpx)

    row_step = per * n_row
    place = cols_v[...] // row_step * per + cols_v[...] % per
    hot = []
    for k in range(2):
        weight = jnp.where(live_v[...] > k, 0.5, 0.0)
        match = lax.broadcasted_iota(jnp.int32, (ncb, nb), 0) == place[k : k + 1]
        hot.append(jnp.where(match, weight, 0.0))
    hot = jnp.concatenate(hot + hot, axis=1).astype(BF16)
    gap = jnp.zeros((width, span), F32)
    gaps = jnp.zeros((LANES - 4 * width, span), F32)
    gram_x = mm(x_now, jnp.concatenate([x_now, gap, p_now, gap, gaps], axis=0), NT)
    gram_p = mm(p_now, jnp.concatenate([gap, gap, gap, p_now, gaps], axis=0), NT)

    def pair_of(b):
        return jnp.concatenate([blk[b, 0], blk[b, 1]], axis=1)

    def flat(panel, r):
        return jnp.concatenate([panel[r, o] for o in range(per)], axis=1)

    def backward(panel):
        def group(r):
            for o in range(per):
                b = r * per + o
                out = fast_mm(split_rows(panel[r, o]), pair_of(b))
                out = out[:width] + out[width:]
                for k in range(2):
                    start = pl.multiple_of((k * nb + b) * width, width)
                    prod[pl.ds(start, width), :] = out[:, k * LANES : (k + 1) * LANES]

        lax.fori_loop(0, n_row, plain(group), 0)
        for vec in range(width):
            part = split_rows(prod[pl.ds(vec, slots, stride=width), :])
            spread[pl.ds(vec, ncb, stride=width), :] = fast_mm(hot, part)

    def forward_group(panel, r):
        outs = []
        for o in range(per):
            b = r * per + o
            picked = []
            for k in range(2):
                g = cols_s[k, b]
                weight = jnp.where(live_s[0, b] > k, 0.5, 0.0)
                picked.append(panel[g // row_step, g % per] * weight)
            out = fast_mm(split_rows(jnp.concatenate(picked, axis=1)), pair_of(b), NT)
            outs.append(out[:width] + out[width:])
        return outs

    def bilinear(left, right):
        high = left.astype(BF16)
        low = (left - high.astype(F32)).astype(BF16)
        rows = jnp.concatenate([high, low], axis=0)
        r_high = right.astype(BF16)
        r_low = (right - r_high.astype(F32)).astype(BF16)
        return fast_mm(
            jnp.concatenate([rows, rows], axis=1), jnp.concatenate([r_high, r_low], axis=1), NT
        )

    def fs_piece(i):
        return fs.at[i]

    def spread_piece(i):
        size = per * width
        return spread.at[pl.ds(pl.multiple_of(i * size, size), size), :]

    gather_relay("row", AGX_ROW, rpx)
    gather_relay("col", AGX_COL, cpx)
    gather_begin("col", AGP_COL, cpp)
    gather_begin("row", AGP_ROW, rpp)
    fetch.wait()
    gather_finish("row", AGX_ROW, rpx)
    backward(rpx)
    scatter_begin("col", RS_COL, spread_piece, ra_col)
    gather_finish("col", AGX_COL, cpx)

    def first_group(r, total):
        outs = forward_group(cpx, r)
        for o in range(per):
            fs[r, o * width : (o + 1) * width, :] = outs[o]
        right = jnp.concatenate([gap, jnp.concatenate(outs, axis=1), gap, gap, gaps], axis=0)
        return total + bilinear(flat(rpx, r), right)

    own_xx = lax.fori_loop(0, n_row, first_group, jnp.zeros((2 * width, LANES), F32))
    scatter_begin("row", RS_ROW, fs_piece, ra_row)
    sum_begin(0, AR1, gram_x + gram_p + (own_xx[:width] + own_xx[width:]))
    scatter_relay("col", RS_COL, spread_piece, ra_col, rb_col)
    scatter_relay("row", RS_ROW, fs_piece, ra_row, rb_row)
    sum_second(0, AR1)
    gather_relay("row", AGP_ROW, rpp)
    sum_third(0, AR1)
    gather_relay("col", AGP_COL, cpp)
    row_x = sum_end(0, AR1)

    lane, sub = lanes_of(width), subs_of(width)
    half_xx = band(row_x, width, 2 * width, -width)
    cross = symmetric(half_xx)
    work = band(row_x, 0, width) + pltpu.roll(cross, 64, 1)
    work = eliminate(work + jnp.where(lane == sub + 96, 1.0, 0.0), 0, width)
    halfway = band(work, 64, 64 + width, -64)
    inverse = band(work, 96, 96 + width, -96)
    coef_t = mm(pad_rows(halfway, LANES).T[:width], pad_rows(inverse, LANES))
    moved = mm(coef_t, pad_rows(x_now, LANES))

    image = scatter_finish("row", RS_ROW, fs_piece, ra_row, rb_row)
    image = image + scatter_finish("col", RS_COL, spread_piece, ra_col, rb_col)
    image = jnp.concatenate([image[o * width : (o + 1) * width] for o in range(per)], axis=1)
    resid = image - moved
    for o in range(per):
        rpr[me_r, o] = resid[:, o * LANES : (o + 1) * LANES]
        cpr[me_c, o] = resid[:, o * LANES : (o + 1) * LANES]
    gather_begin("col", AGR_COL, cpr)
    gather_begin("row", AGR_ROW, rpr)
    resid_ref[...] = resid

    gram_r = mm(resid, jnp.concatenate([x_now, resid, p_now, image, gaps], axis=0), NT)
    right = jnp.concatenate([gap, gap, gap, gap, p_now, gaps[width:]], axis=0)
    sum_begin(1, AR2, gram_r + mm(image, right, NT))
    gather_finish("row", AGP_ROW, rpp)
    gather_finish("col", AGP_COL, cpp)

    def second_group(r):
        outs = forward_group(cpp, r)
        fp[r] = jnp.concatenate(outs, axis=1)

    lax.fori_loop(0, n_row, plain(second_group), 0)
    gather_relay("row", AGR_ROW, rpr)
    gather_relay("col", AGR_COL, cpr)
    sum_second(1, AR2)
    gather_finish("row", AGR_ROW, rpr)
    gather_finish("col", AGR_COL, cpr)
    sum_third(1, AR2)

    def third_group(r, total):
        outs = forward_group(cpr, r)
        right = jnp.concatenate([gap, jnp.concatenate(outs, axis=1), fp[r], gap, gaps], axis=0)
        left = jnp.concatenate([flat(rpr, r), flat(rpp, r)], axis=0)
        return total + bilinear(left, right)

    own = lax.fori_loop(0, n_row, third_group, jnp.zeros((4 * width, LANES), F32))
    own = own[: 2 * width] + own[2 * width :]
    sum_begin(2, AR3, own[:width] + pltpu.roll(own[width:], 64, 1))

    full = 3 * width
    row_r = sum_end(1, AR2)
    lane, sub = lanes_of(full), subs_of(full)
    row_p = band(row_x, 3 * width, 4 * width, -width)
    gram = jnp.concatenate(
        [
            0.5 * band(row_x, 0, width) + band(row_x, 2 * width, full),
            band(row_r, 0, width) + 0.5 * band(row_r, width, 2 * width) + band(row_r, 2 * width, full),
            0.5 * row_p,
        ],
        axis=0,
    )
    edge = jnp.zeros((width, LANES), F32)
    known = symmetric(
        jnp.concatenate(
            [half_xx + band(row_r, 64, 64 + width, -32), band(row_r, full, full + width, -full), edge],
            axis=0,
        )
    )
    work = symmetric(gram) + jnp.where(lane == sub + 64, 1.0, 0.0)
    work = eliminate(work, 0, width)
    sum_second(2, AR3)
    work = eliminate(work, width, 2 * width)
    sum_third(2, AR3)
    work = eliminate(work, 2 * width, full)
    inverse = band(work, 64, 64 + full, -64)
    inverse_pad = pad_rows(inverse, LANES)

    last = sum_end(2, AR3)
    late = jnp.concatenate([edge, band(last, 0, full), band(last, 64, 64 + full, -64)], axis=0)
    middle = known + symmetric(late)

    reduced = mm(mm(inverse, pad_rows(middle, LANES)), inverse_pad, NT)
    reduced_ref[...] = reduced[:, :full]
    shifted = reduced + jnp.where(lane == sub, 3.0, 0.0)
    target_t = mm(shifted[:width], pad_rows(shifted, LANES))
    mixing_t = mm(target_t, inverse_pad)
    gram_new = mm(target_t, pad_rows(target_t, LANES), NT)
    work = band(gram_new, 0, width) + pltpu.roll(mixing_t, 64, 1)
    work = eliminate(work, 0, width)
    final = band(work, 64, 64 + full, -64) * math.sqrt(order_total)
    next_ref[...] = mm(final, pad_rows(jnp.concatenate([x_now, resid, p_now], axis=0), LANES))

    for leave in pending:
        leave()


def per_device(block_vecs, direction, blocks, block_cols, live_counts):
    n_row = lax.axis_size("row")
    n_col = lax.axis_size("col")
    width, span = block_vecs.shape
    per = span // LANES
    nb = blocks.shape[0]
    vmem = pl.BlockSpec(memory_space=pltpu.VMEM)
    smem = pl.BlockSpec(memory_space=pltpu.SMEM)
    hbm = pl.BlockSpec(memory_space=pltpu.HBM)
    block_cols, live_counts = block_cols.T, live_counts.T
    row_panel = pltpu.VMEM((n_row, per, width, LANES), F32)
    col_panel = pltpu.VMEM((n_col, per, width, LANES), F32)
    row_half = pltpu.VMEM((n_row // 2, per * width, LANES), F32)
    col_half = pltpu.VMEM((n_col // 2, per * width, LANES), F32)
    peers = max(n_row, n_col)
    return pl.pallas_call(
        functools.partial(step_kernel, n_row, n_col),
        out_shape=(
            jax.ShapeDtypeStruct((width, span), F32),
            jax.ShapeDtypeStruct((3 * width, 3 * width), F32),
            jax.ShapeDtypeStruct((width, span), F32),
        ),
        in_specs=[hbm, hbm, hbm, smem, smem, vmem, vmem],
        out_specs=(vmem, vmem, vmem),
        scratch_shapes=[
            pltpu.VMEM(blocks.shape, blocks.dtype),
            pltpu.VMEM((width, span), F32),
            pltpu.VMEM((width, span), F32),
            *([row_panel, col_panel] * 3),
            pltpu.VMEM((2 * nb * width, LANES), F32),
            pltpu.VMEM((n_col * per * width, LANES), F32),
            pltpu.VMEM((n_row, per * width, LANES), F32),
            pltpu.VMEM((n_row, width, span), F32),
            row_half,
            row_half,
            col_half,
            col_half,
            pltpu.VMEM((3, n_row // 2, width, LANES), F32),
            pltpu.VMEM((3, n_col // 2, width, LANES), F32),
            pltpu.VMEM((3, 4, width, LANES), F32),
            pltpu.SemaphoreType.DMA((STAGES,)),
            pltpu.SemaphoreType.DMA((STAGES,)),
            pltpu.SemaphoreType.DMA((8, peers // 2)),
            pltpu.SemaphoreType.DMA((3,)),
        ],
        compiler_params=pltpu.CompilerParams(
            collective_id=0, has_side_effects=True, vmem_limit_bytes=63 * 2**20
        ),
    )(block_vecs, direction, blocks, block_cols, live_counts, block_cols, live_counts)


def solution(mesh):
    return jax.shard_map(
        per_device,
        mesh=mesh,
        in_specs=(
            P(None, ("col", "row")),
            P(None, ("col", "row")),
            P("col", "row", None, None),
            P("col", "row"),
            P("col", "row"),
        ),
        out_specs=(P(None, ("col", "row")), P(), P(None, ("col", "row"))),
        check_vma=False,
    )
```

```python
import functools
import math

import jax
import jax.numpy as jnp
from jax import lax
from jax.experimental import pallas as pl
from jax.experimental.pallas import tpu as pltpu
from jax.sharding import PartitionSpec as P

MESH = pl.DeviceIdType.MESH
F32 = jnp.float32
BF16 = jnp.bfloat16
LANES = 128
NT = (((1,), (1,)), ((), ()))
NN = (((1,), (0,)), ((), ()))

AGX_ROW, AGX_COL, AGP_ROW, AGP_COL, AGR_ROW, AGR_COL, RS_ROW, RS_COL = range(0, 16, 2)
AR1, AR2, AR3 = 16, 19, 22
STAGES = 25


def mm(left, right, dims=NN):
    return lax.dot_general(
        left, right, dims, precision=lax.Precision.HIGHEST, preferred_element_type=F32
    )


def fast_mm(left, right, dims=NN):
    return lax.dot_general(left, right, dims, preferred_element_type=F32)


def split_rows(value):
    high = value.astype(BF16)
    low = (value - high.astype(F32)).astype(BF16)
    return jnp.concatenate([high, low], axis=0)


def pad_rows(value, rows):
    return jnp.concatenate(
        [value, jnp.zeros((rows - value.shape[0], value.shape[1]), value.dtype)], axis=0
    )


def lanes_of(rows):
    return lax.broadcasted_iota(jnp.int32, (rows, LANES), 1)


def subs_of(rows):
    return lax.broadcasted_iota(jnp.int32, (rows, LANES), 0)


def eliminate(work, begin, end):
    rows = work.shape[0]
    lane, sub = lanes_of(rows), subs_of(rows)

    def step(k, work):
        row = jnp.sum(jnp.where(sub == k, work, 0.0), axis=0, keepdims=True)
        col = jnp.sum(jnp.where(lane == k, work, 0.0), axis=1, keepdims=True)
        pivot = jnp.sum(jnp.where(lane[:1] == k, row, 0.0), axis=1, keepdims=True)
        inverse = 1.0 / jnp.sqrt(pivot)
        row = row * inverse
        col = col * inverse
        return jnp.where(sub == k, row, jnp.where(sub > k, work - col * row, work))

    return lax.fori_loop(begin, end, step, work)


def symmetric(value):
    return value + pad_rows(value, LANES).T[: value.shape[0]]


def band(value, start, stop, shift=0):
    lane = lanes_of(value.shape[0])
    kept = jnp.where((lane >= start) & (lane < stop), value, 0.0)
    return pltpu.roll(kept, shift % LANES, 1) if shift % LANES else kept


def step_kernel(
    n_row,
    n_col,
    x_hbm,
    p_hbm,
    blocks_hbm,
    cols_s,
    live_s,
    cols_v,
    live_v,
    next_ref,
    reduced_ref,
    resid_ref,
    blk,
    x_ref,
    p_ref,
    rpx,
    cpx,
    rpp,
    cpp,
    rpr,
    cpr,
    prod,
    spread,
    fs,
    fp,
    ra_row,
    rb_row,
    ra_col,
    rb_col,
    sum_row,
    sum_col,
    sum_quad,
    send_sem,
    recv_sem,
    each_sem,
    fetch_sem,
):
    me = {"row": lax.axis_index("row"), "col": lax.axis_index("col")}
    sizes = {"row": n_row, "col": n_col}
    me_r, me_c = me["row"], me["col"]
    twin = {axis: me[axis] + 1 - 2 * lax.rem(me[axis], 2) for axis in me}
    width, span = x_hbm.shape
    per = span // LANES
    nb = blocks_hbm.shape[0]
    ncb = per * n_col
    slots = 2 * nb
    order_total = span * n_row * n_col
    pending = []

    def copy_to(axis, stage, src, dst, peer, single=None):
        return pltpu.make_async_remote_copy(
            src_ref=src,
            dst_ref=dst,
            send_sem=send_sem.at[stage],
            recv_sem=recv_sem.at[stage] if single is None else each_sem.at[stage // 2, single],
            device_id=peer if isinstance(peer, dict) else {axis: peer},
            device_id_type=MESH,
        )

    def whole(stage, buf, count):
        part = buf.at[pl.ds(0, count)]
        return copy_to("row", stage, part, part, twin["row"])

    def alike(axis, first, body, carry=0, base=None):
        n = sizes[axis]
        base = me[axis] if base is None else base
        for d in sorted(range(first, n // 2), key=lambda d: -min(d, n // 2 - d)):
            carry = body(lax.rem(base + 2 * d, n), carry)
        return carry

    def plain(body):
        def run(i, c):
            body(i)
            return c

        return run

    def gather_begin(axis, stage, buf):
        own = buf.at[me[axis]]
        half = sizes[axis] // 2
        alike(
            axis,
            1,
            plain(lambda peer: copy_to(axis, stage, own, own, peer, me[axis] // 2).start()),
        )
        copy_to(axis, stage + 1, own, own, twin[axis]).start()
        if half > 1:
            pending.append(lambda: whole(stage, buf, half - 1).wait_send())
        pending.append(lambda: whole(stage + 1, buf, half).wait_send())

    def gather_relay(axis, stage, buf):
        def relay(source):
            part = buf.at[source]
            copy_to(axis, stage, part, part, source, source // 2).wait_recv()
            copy_to(axis, stage + 1, part, part, twin[axis]).start()

        alike(axis, 1, plain(relay))

    def gather_finish(axis, stage, buf):
        whole(stage + 1, buf, sizes[axis] // 2).wait_recv()

    def scatter_begin(axis, stage, piece, first):
        def to_twin(dest):
            copy_to(
                axis, stage, piece(dest), first.at[dest // 2], twin[axis], dest // 2
            ).start()

        alike(axis, 0, plain(to_twin), base=twin[axis])
        pending.append(lambda: whole(stage, first, sizes[axis] // 2).wait_send())

    def from_twin(axis, stage, piece, first, dest):
        part = first.at[dest // 2]
        copy_to(axis, stage, part, part, twin[axis], dest // 2).wait_recv()
        return piece(dest)[...] + first[dest // 2]

    def scatter_relay(axis, stage, piece, first, second):
        def relay(dest):
            piece(dest)[...] = from_twin(axis, stage, piece, first, dest)
            copy_to(axis, stage + 1, piece(dest), second.at[me[axis] // 2], dest).start()

        alike(axis, 1, plain(relay))
        if sizes[axis] > 2:
            pending.append(lambda: whole(stage + 1, second, sizes[axis] // 2 - 1).wait_send())

    def scatter_finish(axis, stage, piece, first, second):
        total = from_twin(axis, stage, piece, first, me[axis])
        if sizes[axis] > 2:
            whole(stage + 1, second, sizes[axis] // 2 - 1).wait_recv()
        return alike(axis, 1, lambda source, total: total + second[source // 2], total)

    quad = 2 * lax.rem(me_r, 2) + lax.rem(me_c, 2)

    def others():
        for dr, dc in ((1, 1), (0, 1), (1, 0)):
            row = twin["row"] if dr else me_r
            col = twin["col"] if dc else me_c
            yield {"row": row, "col": col}

    def sum_axis_begin(axis, stage, buf, value):
        own = buf.at[me[axis] // 2]
        own[...] = value
        alike(axis, 1, plain(lambda peer: copy_to(axis, stage, own, own, peer).start()))
        if sizes[axis] > 2:
            pending.append(lambda: whole(stage, buf, sizes[axis] // 2 - 1).wait_send())

    def sum_axis_end(axis, stage, buf):
        if sizes[axis] > 2:
            whole(stage, buf, sizes[axis] // 2 - 1).wait_recv()
        total = buf[0]
        for i in range(1, sizes[axis] // 2):
            total = total + buf[i]
        return total

    def sum_begin(which, base, value):
        sum_axis_begin("row", base, sum_row.at[which], value)

    def sum_second(which, base):
        total = sum_axis_end("row", base, sum_row.at[which])
        sum_axis_begin("col", base + 1, sum_col.at[which], total)

    def sum_third(which, base):
        buf = sum_quad.at[which]
        own = buf.at[quad]
        own[...] = sum_axis_end("col", base + 1, sum_col.at[which])
        for peer in others():
            copy_to(None, base + 2, own, own, peer).start()
        pending.append(lambda: whole(base + 2, buf, 3).wait_send())

    def sum_end(which, base):
        buf = sum_quad.at[which]
        whole(base + 2, buf, 3).wait_recv()
        return (buf[0] + buf[1]) + (buf[2] + buf[3])

    fetch = pltpu.make_async_copy(blocks_hbm, blk, fetch_sem.at[0])
    fetch_x = pltpu.make_async_copy(x_hbm, x_ref, fetch_sem.at[1])
    fetch_p = pltpu.make_async_copy(p_hbm, p_ref, fetch_sem.at[2])
    fetch_x.start()
    fetch_p.start()
    barrier = pltpu.get_barrier_semaphore()

    def greet(peer):
        pl.semaphore_signal(barrier, inc=1, device_id=peer, device_id_type=MESH)

    for axis in ("row", "col"):
        alike(axis, 1, plain(lambda peer, axis=axis: greet({axis: peer})))
    for peer in others():
        greet(peer)
    fetch.start()

    fetch_x.wait()
    fetch_p.wait()
    x_now = x_ref[...]
    p_now = p_ref[...]
    for o in range(per):
        rpx[me_r, o] = x_now[:, o * LANES : (o + 1) * LANES]
        cpx[me_c, o] = x_now[:, o * LANES : (o + 1) * LANES]
        rpp[me_r, o] = p_now[:, o * LANES : (o + 1) * LANES]
        cpp[me_c, o] = p_now[:, o * LANES : (o + 1) * LANES]
    pl.semaphore_wait(barrier, n_row // 2 + n_col // 2 + 1)

    gather_begin("col", AGX_COL, cpx)
    gather_begin("row", AGX_ROW, rpx)

    row_step = per * n_row
    place = cols_v[...] // row_step * per + cols_v[...] % per
    hot = []
    for k in range(2):
        weight = jnp.where(live_v[...] > k, 0.5, 0.0)
        match = lax.broadcasted_iota(jnp.int32, (ncb, nb), 0) == place[k : k + 1]
        hot.append(jnp.where(match, weight, 0.0))
    hot = jnp.concatenate(hot + hot, axis=1).astype(BF16)
    gap = jnp.zeros((width, span), F32)
    gaps = jnp.zeros((LANES - 4 * width, span), F32)
    gram_x = mm(x_now, jnp.concatenate([x_now, gap, p_now, gap, gaps], axis=0), NT)
    gram_p = mm(p_now, jnp.concatenate([gap, gap, gap, p_now, gaps], axis=0), NT)

    def pair_of(b):
        return jnp.concatenate([blk[b, 0], blk[b, 1]], axis=1)

    def flat(panel, r):
        return jnp.concatenate([panel[r, o] for o in range(per)], axis=1)

    def backward(panel):
        def group(r):
            for o in range(per):
                b = r * per + o
                out = fast_mm(split_rows(panel[r, o]), pair_of(b))
                out = out[:width] + out[width:]
                for k in range(2):
                    start = pl.multiple_of((k * nb + b) * width, width)
                    prod[pl.ds(start, width), :] = out[:, k * LANES : (k + 1) * LANES]

        lax.fori_loop(0, n_row, plain(group), 0, unroll=4)
        for vec in range(width):
            part = split_rows(prod[pl.ds(vec, slots, stride=width), :])
            spread[pl.ds(vec, ncb, stride=width), :] = fast_mm(hot, part)

    def forward_group(panel, r):
        outs = []
        for o in range(per):
            b = r * per + o
            picked = []
            for k in range(2):
                g = cols_s[k, b]
                weight = jnp.where(live_s[0, b] > k, 0.5, 0.0)
                picked.append(panel[g // row_step, g % per] * weight)
            out = fast_mm(split_rows(jnp.concatenate(picked, axis=1)), pair_of(b), NT)
            outs.append(out[:width] + out[width:])
        return outs

    def bilinear(left, right):
        high = left.astype(BF16)
        low = (left - high.astype(F32)).astype(BF16)
        rows = jnp.concatenate([high, low], axis=0)
        r_high = right.astype(BF16)
        r_low = (right - r_high.astype(F32)).astype(BF16)
        return fast_mm(
            jnp.concatenate([rows, rows], axis=1), jnp.concatenate([r_high, r_low], axis=1), NT
        )

    def fs_piece(i):
        return fs.at[i]

    def spread_piece(i):
        size = per * width
        return spread.at[pl.ds(pl.multiple_of(i * size, size), size), :]

    gather_relay("row", AGX_ROW, rpx)
    gather_relay("col", AGX_COL, cpx)
    gather_begin("col", AGP_COL, cpp)
    gather_begin("row", AGP_ROW, rpp)
    fetch.wait()
    gather_finish("row", AGX_ROW, rpx)
    backward(rpx)
    scatter_begin("col", RS_COL, spread_piece, ra_col)
    gather_finish("col", AGX_COL, cpx)

    def first_group(r, total):
        outs = forward_group(cpx, r)
        for o in range(per):
            fs[r, o * width : (o + 1) * width, :] = outs[o]
        right = jnp.concatenate([gap, jnp.concatenate(outs, axis=1), gap, gap, gaps], axis=0)
        return total + bilinear(flat(rpx, r), right)

    own_xx = lax.fori_loop(0, n_row, first_group, jnp.zeros((2 * width, LANES), F32), unroll=4)
    scatter_begin("row", RS_ROW, fs_piece, ra_row)
    sum_begin(0, AR1, gram_x + gram_p + (own_xx[:width] + own_xx[width:]))
    scatter_relay("col", RS_COL, spread_piece, ra_col, rb_col)
    sum_second(0, AR1)
    scatter_relay("row", RS_ROW, fs_piece, ra_row, rb_row)
    sum_third(0, AR1)
    gather_relay("row", AGP_ROW, rpp)
    gather_relay("col", AGP_COL, cpp)
    row_x = sum_end(0, AR1)

    lane, sub = lanes_of(width), subs_of(width)
    half_xx = band(row_x, width, 2 * width, -width)
    cross = symmetric(half_xx)
    work = band(row_x, 0, width) + pltpu.roll(cross, 64, 1)
    work = eliminate(work + jnp.where(lane == sub + 96, 1.0, 0.0), 0, width)
    halfway = band(work, 64, 64 + width, -64)
    inverse = band(work, 96, 96 + width, -96)
    coef_t = mm(pad_rows(halfway, LANES).T[:width], pad_rows(inverse, LANES))
    moved = mm(coef_t, pad_rows(x_now, LANES))

    image = scatter_finish("row", RS_ROW, fs_piece, ra_row, rb_row)
    image = image + scatter_finish("col", RS_COL, spread_piece, ra_col, rb_col)
    image = jnp.concatenate([image[o * width : (o + 1) * width] for o in range(per)], axis=1)
    resid = image - moved
    for o in range(per):
        rpr[me_r, o] = resid[:, o * LANES : (o + 1) * LANES]
        cpr[me_c, o] = resid[:, o * LANES : (o + 1) * LANES]
    gather_begin("col", AGR_COL, cpr)
    gather_begin("row", AGR_ROW, rpr)
    resid_ref[...] = resid

    gram_r = mm(resid, jnp.concatenate([x_now, resid, p_now, image, gaps], axis=0), NT)
    right = jnp.concatenate([gap, gap, gap, gap, p_now, gaps[width:]], axis=0)
    sum_begin(1, AR2, gram_r + mm(image, right, NT))
    gather_finish("row", AGP_ROW, rpp)
    gather_finish("col", AGP_COL, cpp)

    def second_group(r):
        outs = forward_group(cpp, r)
        fp[r] = jnp.concatenate(outs, axis=1)

    lax.fori_loop(0, n_row, plain(second_group), 0, unroll=4)
    gather_relay("row", AGR_ROW, rpr)
    gather_relay("col", AGR_COL, cpr)
    sum_second(1, AR2)
    gather_finish("row", AGR_ROW, rpr)
    gather_finish("col", AGR_COL, cpr)
    sum_third(1, AR2)

    def third_group(r, total):
        outs = forward_group(cpr, r)
        right = jnp.concatenate([gap, jnp.concatenate(outs, axis=1), fp[r], gap, gaps], axis=0)
        left = jnp.concatenate([flat(rpr, r), flat(rpp, r)], axis=0)
        return total + bilinear(left, right)

    own = lax.fori_loop(0, n_row, third_group, jnp.zeros((4 * width, LANES), F32), unroll=4)
    own = own[: 2 * width] + own[2 * width :]
    sum_begin(2, AR3, own[:width] + pltpu.roll(own[width:], 64, 1))

    full = 3 * width
    row_r = sum_end(1, AR2)
    lane, sub = lanes_of(full), subs_of(full)
    row_p = band(row_x, 3 * width, 4 * width, -width)
    gram = jnp.concatenate(
        [
            0.5 * band(row_x, 0, width) + band(row_x, 2 * width, full),
            band(row_r, 0, width) + 0.5 * band(row_r, width, 2 * width) + band(row_r, 2 * width, full),
            0.5 * row_p,
        ],
        axis=0,
    )
    edge = jnp.zeros((width, LANES), F32)
    known = symmetric(
        jnp.concatenate(
            [half_xx + band(row_r, 64, 64 + width, -32), band(row_r, full, full + width, -full), edge],
            axis=0,
        )
    )
    work = symmetric(gram) + jnp.where(lane == sub + 64, 1.0, 0.0)
    work = eliminate(work, 0, width)
    sum_second(2, AR3)
    work = eliminate(work, width, 2 * width)
    sum_third(2, AR3)
    work = eliminate(work, 2 * width, full)
    inverse = band(work, 64, 64 + full, -64)
    inverse_pad = pad_rows(inverse, LANES)

    last = sum_end(2, AR3)
    late = jnp.concatenate([edge, band(last, 0, full), band(last, 64, 64 + full, -64)], axis=0)
    middle = known + symmetric(late)

    reduced = mm(mm(inverse, pad_rows(middle, LANES)), inverse_pad, NT)
    reduced_ref[...] = reduced[:, :full]
    shifted = reduced + jnp.where(lane == sub, 3.0, 0.0)
    target_t = mm(shifted[:width], pad_rows(shifted, LANES))
    mixing_t = mm(target_t, inverse_pad)
    gram_new = mm(target_t, pad_rows(target_t, LANES), NT)
    work = band(gram_new, 0, width) + pltpu.roll(mixing_t, 64, 1)
    work = eliminate(work, 0, width)
    final = band(work, 64, 64 + full, -64) * math.sqrt(order_total)
    next_ref[...] = mm(final, pad_rows(jnp.concatenate([x_now, resid, p_now], axis=0), LANES))

    for leave in pending:
        leave()


def per_device(block_vecs, direction, blocks, block_cols, live_counts):
    n_row = lax.axis_size("row")
    n_col = lax.axis_size("col")
    width, span = block_vecs.shape
    per = span // LANES
    nb = blocks.shape[0]
    vmem = pl.BlockSpec(memory_space=pltpu.VMEM)
    smem = pl.BlockSpec(memory_space=pltpu.SMEM)
    hbm = pl.BlockSpec(memory_space=pltpu.HBM)
    block_cols, live_counts = block_cols.T, live_counts.T
    row_panel = pltpu.VMEM((n_row, per, width, LANES), F32)
    col_panel = pltpu.VMEM((n_col, per, width, LANES), F32)
    row_half = pltpu.VMEM((n_row // 2, per * width, LANES), F32)
    col_half = pltpu.VMEM((n_col // 2, per * width, LANES), F32)
    peers = max(n_row, n_col)
    return pl.pallas_call(
        functools.partial(step_kernel, n_row, n_col),
        out_shape=(
            jax.ShapeDtypeStruct((width, span), F32),
            jax.ShapeDtypeStruct((3 * width, 3 * width), F32),
            jax.ShapeDtypeStruct((width, span), F32),
        ),
        in_specs=[hbm, hbm, hbm, smem, smem, vmem, vmem],
        out_specs=(vmem, vmem, vmem),
        scratch_shapes=[
            pltpu.VMEM(blocks.shape, blocks.dtype),
            pltpu.VMEM((width, span), F32),
            pltpu.VMEM((width, span), F32),
            *([row_panel, col_panel] * 3),
            pltpu.VMEM((2 * nb * width, LANES), F32),
            pltpu.VMEM((n_col * per * width, LANES), F32),
            pltpu.VMEM((n_row, per * width, LANES), F32),
            pltpu.VMEM((n_row, width, span), F32),
            row_half,
            row_half,
            col_half,
            col_half,
            pltpu.VMEM((3, n_row // 2, width, LANES), F32),
            pltpu.VMEM((3, n_col // 2, width, LANES), F32),
            pltpu.VMEM((3, 4, width, LANES), F32),
            pltpu.SemaphoreType.DMA((STAGES,)),
            pltpu.SemaphoreType.DMA((STAGES,)),
            pltpu.SemaphoreType.DMA((8, peers // 2)),
            pltpu.SemaphoreType.DMA((3,)),
        ],
        compiler_params=pltpu.CompilerParams(
            collective_id=0, has_side_effects=True, vmem_limit_bytes=63 * 2**20
        ),
    )(block_vecs, direction, blocks, block_cols, live_counts, block_cols, live_counts)


def solution(mesh):
    return jax.shard_map(
        per_device,
        mesh=mesh,
        in_specs=(
            P(None, ("col", "row")),
            P(None, ("col", "row")),
            P("col", "row", None, None),
            P("col", "row"),
            P("col", "row"),
        ),
        out_specs=(P(None, ("col", "row")), P(), P(None, ("col", "row"))),
        check_vma=False,
    )
```
